32 devices in a mesh: seq: 4 (over z), exp: 8 (over y, x, core).
Axes of the slice: x: 2, y: 2, z: 4, core: 2. Of those that a mesh axis runs over, the one named last changes fastest.
Arguments:
- queries: bfloat16 [8, 256, 4096], P('exp', 'seq'), may hold values from -30 to 30
- key_heads: bfloat16 [8, 256, 512], P('exp', 'seq'), may hold values from -12 to 12
- value_heads: bfloat16 [8, 256, 512], P('exp', 'seq'), may hold values from -6 to 6
- residual: bfloat16 [8, 256, 4096], P('exp', 'seq'), may hold values from -16 to 16
- lengths: int32 [8, 6], P('exp'), may hold values from 1 to 128, 256 in all within a row
- routes: int32 [8, 256, 4], P('exp', 'seq'), may hold values from 0 to 7, all different within a row; in each aligned block of 64 rows (0 to 63, 64 to 127, ..., all dimensions but the last counted through in order) at most 40 rows name the same one
- gate_weights: bfloat16 [8, 256, 8], P('exp', 'seq'), may hold values from 0.049804688 to 0.29882812
- out_weight: bfloat16 [4096, 4096], P('seq', 'exp'), may hold values from -0.09375 to 0.09375
- norm_gain: float32 [4096], replicated, may hold values from 0.5 to 1.5
- w_gate: bfloat16 [8, 4, 4096, 768], P('exp', 'seq'), may hold values from -0.09375 to 0.09375
- w_up: bfloat16 [8, 4, 4096, 768], P('exp', 'seq'), may hold values from -0.09375 to 0.09375
- w_down: bfloat16 [8, 4, 768, 4096], P('exp', 'seq'), may hold values from -0.15625 to 0.15625
Outputs:
- result: bfloat16 [8, 256, 4096], P('exp', 'seq')
The draws below stay inside these ranges and needn't reach their ends.
Inputs may be any that keep to these rules, and one draw needn't show every extreme that they name: `lengths`: each row sums to 256, and its largest entry is 128. `routes`: the 4 entries of a token differ; among the rows of one device no column is named more than 40 times, a bound that some block reaches.
All inputs are finite; a program needn't handle non-finite values.
Results may differ from the reference program's by a relative error of at most 0.008.
Values may be sent and summed in bfloat16 or wider, within the bound.
A program may use at most 128 MiB of HBM per device.

```python
import math
import jax
import jax.numpy as jnp
import numpy as np
from jax import lax

D = 4096
HQ = 32
KV_HEADS = 4
HEAD_DIM = 128
FF = 1536
EXP_COL = 2
NODES_TOK = 4
EPISODES = 6
TOK_DEV = 64
LENGTH = 256
PACKS = 8
MOST_LEN = 128
CAP = 40
TOP = 8
FF_PART = 768
N_SEQ = 4
N_EXP = 8


def draw_queries(key, part):
    noise_key = jax.random.fold_in(key, 11)
    drawn = jnp.clip(jax.random.normal(noise_key, (PACKS, LENGTH, HQ * HEAD_DIM), jnp.float32), -6.0, 6.0)
    return drawn.astype(jnp.bfloat16)


def draw_key_heads(key, part):
    noise_key = jax.random.fold_in(key, 12)
    drawn = jnp.clip(jax.random.normal(noise_key, (PACKS, LENGTH, KV_HEADS * HEAD_DIM), jnp.float32), -6.0, 6.0)
    return drawn.astype(jnp.bfloat16)


def draw_residual(key, part):
    noise_key = jax.random.fold_in(key, 21)
    drawn = jnp.clip(jax.random.normal(noise_key, (PACKS, LENGTH, D), jnp.float32), -6.0, 6.0)
    return drawn.astype(jnp.bfloat16)


def level_of(rng, dims, pieces, least, largest):
    gain = 1.0
    for dim, parts in pieces:
        heights = jax.random.uniform(jax.random.fold_in(jax.random.fold_in(rng, 6), dim), (parts,), jnp.float32, least / len(pieces), largest / len(pieces))
        gain = gain * jnp.repeat(jnp.exp(heights), dims[dim] // parts).reshape((-1,) + (1,) * (len(dims) - 1 - dim))
    return gain


def length_profile(count, total, reach, skew):
    weights = [(1 << 20) // math.isqrt(standing ** skew) + 1 for standing in range(2, count + 1)]
    surplus, holding = total - reach - (count - 1), [1] * (count - 1)
    while surplus > 0:
        movable = [i for i in range(count - 1) if holding[i] < reach]
        mass, left = sum([weights[i] for i in movable]), surplus
        for i in movable:
            addition = min(reach - holding[i], max(1, left * weights[i] // mass), surplus)
            holding[i] = holding[i] + addition
            surplus = surplus - addition
    return np.array([reach] + holding)


def ragged(own_key, amount, total, reach, skew):
    if amount == 2:
        one = jax.random.randint(own_key, (), max(1, total - reach), min(reach, total - 1) + 1)
        return jnp.stack([one, total - one])
    tallies = jnp.asarray(length_profile(amount, total, reach, skew), jnp.int32)
    twos = (amount - 1) // 2
    source_of, sink = tallies[1:1 + 2 * twos:2], tallies[2:2 + 2 * twos:2]
    room = jnp.minimum(source_of - 1, reach - sink)
    moved = jax.random.randint(jax.random.fold_in(own_key, 1), (twos,), 0, 1 << 20) % (room + 1)
    tallies = tallies.at[1:1 + 2 * twos:2].set(source_of - moved).at[2:2 + 2 * twos:2].set(sink + moved)
    return tallies[jax.random.permutation(jax.random.fold_in(own_key, 2), amount)]


def assign_block(rng, own, number, rows, amount, top, limit, skew):
    order = jax.random.permutation(rng, amount)
    packed, ordinary = shares(amount, rows * top, limit, skew, True), shares(amount, rows * top, limit, skew, False)
    places = jnp.arange(amount)

    def named(sizes, rotation):
        used = int((sizes > 0).sum())
        fixed = max(1, used // 4)
        passed = fixed + (places - fixed + rotation * (used - fixed)) % max(1, amount - fixed)
        return jnp.zeros((amount,), jnp.int32).at[order[jnp.where(places < fixed, places, passed)]].set(jnp.asarray(sizes, jnp.int32))

    sizes = jnp.where(number % 4 == 0, named(packed, number // 4), named(ordinary, number - number // 4 - 1))
    mixed = jax.random.permutation(jax.random.fold_in(own, 3), amount)
    source_of, taker = mixed[0:amount // 2 * 2:2], mixed[1:amount // 2 * 2:2]
    margin = jnp.minimum(sizes[source_of] - 1, limit - sizes[taker]) // 2
    margin = jnp.where((source_of == order[0]) | (taker == order[0]) | (sizes[taker] == 0), 0, jnp.maximum(margin, 0))
    passed = jax.random.randint(jax.random.fold_in(own, 4), (amount // 2,), 0, 1 << 20) % (margin + 1)
    sizes = sizes.at[source_of].add(-passed).at[taker].add(passed)
    members = jnp.searchsorted(jnp.cumsum(sizes), jnp.arange(rows * top), side="right").astype(jnp.int32)
    table = members.reshape(top, rows).T
    table = table[jax.random.permutation(jax.random.fold_in(own, 1), rows)]
    rotation = jax.random.randint(jax.random.fold_in(own, 2), (rows, 1), 0, top)
    return jnp.take_along_axis(table, (jnp.arange(top)[None, :] + rotation) % top, axis=1)


def shares(number_of, total, limit, skew, full):
    portions = [(1 << 20) // math.isqrt(rank ** skew) + 1 for rank in range(1, number_of + 1)]
    largest = limit if full else min(limit, max(-(-total // number_of), total * portions[0] // sum(portions)))
    least = 1 if total - largest >= number_of - 1 else 0
    counts, spare = [largest] + [least] * (number_of - 1), total - largest - least * (number_of - 1)
    while spare > 0:
        free = [i for i in range(1, number_of) if counts[i] < largest] or [i for i in range(1, number_of) if counts[i] < limit]
        whole, left = sum([portions[i] for i in free]), spare
        for i in free:
            addition = min(limit - counts[i], max(1, left * portions[i] // whole), spare)
            counts[i] = counts[i] + addition
            spare = spare - addition
    return np.array(counts)


def bell_draw(rng, extent, scale, limit, cuts=(), kind=jnp.bfloat16):
    drawn = jax.random.normal(rng, extent, jnp.float32) * scale
    if len(cuts) > 0:
        drawn = level_of(rng, extent, cuts, -0.22, 0.18) * drawn
    return jnp.clip(drawn, min=-limit, max=limit).astype(kind)


def setup_inputs(seed: int = 0) -> dict:
    seeds = jax.random.split(jax.random.key(seed), 13)
    queries = draw_queries(jax.random.fold_in(seeds[12], 71), 0)
    key_heads = draw_key_heads(jax.random.fold_in(seeds[12], 71), 0)
    value_heads = bell_draw(seeds[2], (PACKS, LENGTH, KV_HEADS * HEAD_DIM), 1.0, 6.0, ((0, 8), (1, 4)))
    residual = draw_residual(jax.random.fold_in(seeds[12], 71), 0)
    lengths = jax.vmap(lambda own: ragged(own, EPISODES, LENGTH, MOST_LEN, 2))(jax.random.split(seeds[4], PACKS)).reshape((PACKS, EPISODES)).astype(jnp.int32)
    routes_keys = jax.random.split(jax.random.fold_in(seeds[5], 1), PACKS * LENGTH // TOK_DEV)
    routes_turns = jax.random.permutation(jax.random.fold_in(seeds[5], 3), PACKS * LENGTH // TOK_DEV)
    routes = jax.vmap(lambda own, number: assign_block(jax.random.fold_in(seeds[5], 2), own, number, TOK_DEV, N_EXP, NODES_TOK, CAP, 2))(routes_keys, routes_turns).reshape((PACKS, LENGTH, NODES_TOK))
    gate_weights = jnp.clip(0.049804688 + 0.24902344 * jax.random.uniform(seeds[6], (PACKS, LENGTH, TOP), jnp.float32) ** level_of(seeds[6], (PACKS, LENGTH, TOP), ((0, 8), (1, 4)), -0.2, 0.2), 0.049804688, 0.29882812).astype(jnp.bfloat16)
    out_weight = bell_draw(seeds[7], (HQ * HEAD_DIM, D), (HQ * HEAD_DIM) ** -0.5, 0.09375, ((0, 4), (1, 8)))
    norm_gain = jnp.clip(1.0 + 0.1 * jax.random.normal(seeds[8], (D,), jnp.float32), 0.5, 1.5)
    w_gate = bell_draw(seeds[9], (N_EXP, N_SEQ, D, FF_PART), D ** -0.5, 0.09375, ((0, 8), (1, 4)))
    w_up = bell_draw(seeds[10], (N_EXP, N_SEQ, D, FF_PART), D ** -0.5, 0.09375, ((0, 8), (1, 4)))
    w_down = bell_draw(seeds[11], (N_EXP, N_SEQ, FF_PART, D), FF ** -0.5, 0.15625, ((0, 8), (1, 4)))
    return dict(queries=queries, key_heads=key_heads, value_heads=value_heads, residual=residual, lengths=lengths, routes=routes, gate_weights=gate_weights, out_weight=out_weight, norm_gain=norm_gain, w_gate=w_gate, w_up=w_up, w_down=w_down)


epsilon = 1e-06

def episode_ids(length_row, position_count):
    bounds = jnp.cumsum(length_row)
    position = jnp.arange(position_count, dtype=jnp.int32)
    return lax.optimization_barrier(jnp.sum((position[:, None] >= bounds[None, :]).astype(jnp.int32), axis=1))

def attend(query_rows, key_rows, value_rows, episode):
    row_count = query_rows.shape[0]
    groups = key_rows.shape[1] // HEAD_DIM
    per_group = query_rows.shape[1] // HEAD_DIM // groups
    q_heads = query_rows.astype(jnp.float32).reshape(row_count, groups, per_group, HEAD_DIM)
    k_heads = key_rows.astype(jnp.float32).reshape(row_count, groups, HEAD_DIM)
    v_heads = value_rows.astype(jnp.float32).reshape(row_count, groups, HEAD_DIM)
    scores = jnp.einsum('tgpd,ugd->gptu', q_heads, k_heads) / math.sqrt(HEAD_DIM)
    position = jnp.arange(row_count, dtype=jnp.int32)
    allowed = (episode[:, None] == episode[None, :]) & (position[None, :] <= position[:, None])
    scores = jnp.where(allowed, scores, -jnp.inf)
    row_maximum = lax.optimization_barrier(jnp.max(scores, axis=-1, keepdims=True))
    weights = jnp.exp(scores - row_maximum)
    probability = (weights / lax.optimization_barrier(jnp.sum(weights, axis=-1, keepdims=True))).astype(jnp.bfloat16)
    mixed = jnp.einsum('gptu,ugd->tgpd', probability.astype(jnp.float32), v_heads)
    return mixed.astype(jnp.bfloat16).reshape(row_count, groups * per_group * HEAD_DIM)

def reference(queries, key_heads, value_heads, residual, lengths, routes, gate_weights, out_weight, norm_gain, w_gate, w_up, w_down):

    def one_pack(pack_args):
        query_rows, key_rows, value_rows, length_row = pack_args
        return attend(query_rows, key_rows, value_rows, episode_ids(length_row, LENGTH))
    mixed = lax.map(one_pack, (queries, key_heads, value_heads, lengths))
    projected = jnp.dot(mixed.reshape(-1, HQ * HEAD_DIM), out_weight, preferred_element_type=jnp.float32)
    hidden = residual.reshape(-1, D).astype(jnp.float32) + projected
    inverse = lax.rsqrt(lax.optimization_barrier(jnp.mean(hidden * hidden, axis=1, keepdims=True)) + epsilon)
    normalized_rows = (hidden * inverse * norm_gain[None, :]).astype(jnp.bfloat16)
    routed = routes.reshape(-1, NODES_TOK)
    gate_pair = gate_weights.reshape(-1, NODES_TOK, EXP_COL).astype(jnp.float32)
    token_total = routed.shape[0]
    slot_limit = CAP * N_SEQ * N_EXP
    halves = N_SEQ // EXP_COL

    def column(carry_sum, column_id):
        on_node = routed == column_id
        member = jnp.any(on_node, axis=1)
        rank = jnp.cumsum(member.astype(jnp.int32)) - 1
        slot = jnp.where(member, rank, slot_limit)
        row_index = jnp.zeros((slot_limit + 1,), jnp.int32).at[slot].set(jnp.arange(token_total, dtype=jnp.int32))[:slot_limit]
        valid_slot = jnp.zeros((slot_limit + 1,), jnp.float32).at[slot].set(1.0)[:slot_limit]
        token_rows = normalized_rows[row_index]
        node_route_gate = lax.optimization_barrier(jnp.sum(jnp.where(on_node[:, :, None], gate_pair, 0.0), axis=1))[row_index]
        gate_block = w_gate[column_id]
        up_block = w_up[column_id]
        down_block = w_down[column_id]
        accum_sum = jnp.zeros((slot_limit, D), jnp.float32)
        for expert_slot in range(EXP_COL):
            for half_slot in range(halves):
                entry = expert_slot * halves + half_slot
                gate_proj = jnp.dot(token_rows, gate_block[entry], preferred_element_type=jnp.float32)
                up_proj = jnp.dot(token_rows, up_block[entry], preferred_element_type=jnp.float32)
                activated = (jax.nn.silu(gate_proj) * up_proj).astype(jnp.bfloat16)
                partial_value = jnp.dot(activated, down_block[entry], preferred_element_type=jnp.float32).astype(jnp.bfloat16)
                partial_value = lax.optimization_barrier(partial_value)
                weighted = (partial_value.astype(jnp.float32) * node_route_gate[:, expert_slot:expert_slot + 1]).astype(jnp.bfloat16)
                weighted = lax.optimization_barrier(weighted)
                accum_sum = accum_sum + weighted.astype(jnp.float32)
        node_sum = lax.optimization_barrier(accum_sum.astype(jnp.bfloat16))
        node_sum = node_sum.astype(jnp.float32) * valid_slot[:, None]
        return (carry_sum.at[row_index].add(node_sum), None)
    mixture_expert_total, _ = lax.scan(column, jnp.zeros((token_total, D), jnp.float32), jnp.arange(N_EXP, dtype=jnp.int32))
    return (hidden + mixture_expert_total).astype(jnp.bfloat16).reshape(PACKS, LENGTH, D)
```

```python
import functools
import math

import jax
import jax.numpy as jnp
from jax import lax
from jax.experimental import pallas as pl
from jax.experimental.pallas import tpu as pltpu
from jax.sharding import PartitionSpec as P

HEAD_DIM = 128
EXP_COL = 2


epsilon = 1e-06


def episode_ids(length_row, position_count):
    bounds = jnp.cumsum(length_row)
    position = jnp.arange(position_count, dtype=jnp.int32)
    return jnp.sum((position[:, None] >= bounds[None, :]).astype(jnp.int32), axis=1)


def attend(query_rows, key_rows, value_rows, episode):
    row_count = query_rows.shape[0]
    groups = key_rows.shape[1] // HEAD_DIM
    per_group = query_rows.shape[1] // HEAD_DIM // groups
    q_heads = query_rows.reshape(row_count, groups, per_group, HEAD_DIM)
    k_heads = key_rows.reshape(row_count, groups, HEAD_DIM)
    v_heads = value_rows.reshape(row_count, groups, HEAD_DIM)
    scores = jnp.einsum(
        "tgpd,ugd->gptu", q_heads, k_heads, preferred_element_type=jnp.float32
    ) / math.sqrt(HEAD_DIM)
    position = jnp.arange(row_count, dtype=jnp.int32)
    allowed = (episode[:, None] == episode[None, :]) & (position[None, :] <= position[:, None])
    scores = jnp.where(allowed, scores, -jnp.inf)
    row_maximum = jnp.max(scores, axis=-1, keepdims=True)
    weights = jnp.exp(scores - row_maximum)
    probability = (weights / jnp.sum(weights, axis=-1, keepdims=True)).astype(jnp.bfloat16)
    mixed = jnp.einsum("gptu,ugd->tgpd", probability, v_heads, preferred_element_type=jnp.float32)
    return mixed.astype(jnp.bfloat16).reshape(row_count, groups * per_group * HEAD_DIM)


def local_routed(
    queries,
    key_heads,
    value_heads,
    residual,
    lengths,
    routes,
    gate_weights,
    out_weight,
    norm_gain,
    w_gate,
    w_up,
    w_down,
):
    seq_count = lax.axis_size("seq")
    columns = lax.axis_size("exp")
    token_count = residual.shape[1]
    model_width = residual.shape[2]
    whole_q, whole_k, whole_v = (
        lax.all_to_all(queries[0], "seq", split_axis=1, concat_axis=0, tiled=True),
        lax.all_to_all(key_heads[0], "seq", split_axis=1, concat_axis=0, tiled=True),
        lax.all_to_all(value_heads[0], "seq", split_axis=1, concat_axis=0, tiled=True),
    )
    episode = episode_ids(lengths[0], whole_q.shape[0])
    mixed = attend(whole_q, whole_k, whole_v, episode)
    head_partial = jnp.dot(
        mixed,
        lax.all_gather(out_weight, "exp", axis=1, tiled=True),
        preferred_element_type=jnp.float32,
    )
    projected = lax.psum_scatter(
        head_partial.astype(jnp.bfloat16), "seq", scatter_dimension=0, tiled=True
    ).astype(jnp.float32)
    hidden = residual[0].astype(jnp.float32) + projected
    inverse = lax.rsqrt(jnp.mean(hidden * hidden, axis=1, keepdims=True) + epsilon)
    normalized_rows = (hidden * inverse * norm_gain[None, :]).astype(jnp.bfloat16)
    routed = routes[0]
    node_count = routed.shape[1]
    capacity = max(2, 5 * token_count * node_count // (4 * columns))
    on_node = routed[:, :, None] == jnp.arange(columns, dtype=jnp.int32)[None, None, :]
    member = jnp.sum(on_node.astype(jnp.int32), axis=1)
    before = jnp.cumsum(member, axis=0) - member
    slot_lookup_index = (
        before[:, :, None] == jnp.arange(capacity, dtype=jnp.int32)[None, None, :]
    ) & (member[:, :, None] > 0)
    slot_flag_mask = slot_lookup_index.astype(jnp.bfloat16)
    outbound = jnp.einsum(
        "roj,rm->ojm", slot_flag_mask, normalized_rows, preferred_element_type=jnp.float32
    ).astype(jnp.bfloat16)
    gate_pair = gate_weights[0].reshape(token_count, node_count, EXP_COL).astype(jnp.float32)
    node_route_gate = jnp.einsum(
        "tnc,tne->tce", on_node.astype(jnp.float32), gate_pair, precision=lax.Precision.HIGHEST
    )
    slot_gate = jnp.einsum(
        "qnr,qny->nry",
        slot_lookup_index.astype(jnp.float32),
        node_route_gate,
        precision=lax.Precision.HIGHEST,
    ).astype(jnp.bfloat16)
    rows_in, gate_in = (
        lax.all_to_all(outbound, "exp", split_axis=0, concat_axis=0, tiled=True),
        lax.all_to_all(slot_gate, "exp", split_axis=0, concat_axis=0, tiled=True),
    )
    rows_all, gate_all = (
        lax.all_gather(rows_in, "seq", axis=0, tiled=True),
        lax.all_gather(gate_in, "seq", axis=0, tiled=True),
    )
    halves = seq_count // EXP_COL
    expert_pick = lax.axis_index("seq") // halves
    flat_rows = rows_all.reshape(-1, model_width)
    flat_gate = lax.dynamic_index_in_dim(
        gate_all.reshape(-1, EXP_COL), expert_pick, axis=1, keepdims=False
    )
    gate_block = w_gate[0, 0]
    up_block = w_up[0, 0]
    down_block = w_down[0, 0]
    gate_proj = jnp.dot(flat_rows, gate_block, preferred_element_type=jnp.float32)
    up_proj = jnp.dot(flat_rows, up_block, preferred_element_type=jnp.float32)
    activated = (jax.nn.silu(gate_proj) * up_proj).astype(jnp.bfloat16)
    partial_value = jnp.dot(activated, down_block, preferred_element_type=jnp.float32).astype(
        jnp.bfloat16
    )
    partial_value = lax.optimization_barrier(partial_value)
    node_sum = lax.psum_scatter(
        (partial_value.astype(jnp.float32) * flat_gate.astype(jnp.float32)[:, None]).astype(
            jnp.bfloat16
        ),
        "seq",
        scatter_dimension=0,
        tiled=True,
    )
    gathered_output = lax.all_to_all(
        node_sum.reshape(columns, capacity, model_width),
        "exp",
        split_axis=0,
        concat_axis=0,
        tiled=True,
    )
    mixture_expert_total = jnp.einsum(
        "gyr,yre->ge", slot_flag_mask, gathered_output, preferred_element_type=jnp.float32
    )
    return (hidden + mixture_expert_total).astype(jnp.bfloat16)[None]

CORE, X_BIT, Y_BIT = 1, 2, 4
ROWS = 16
MESH = pl.DeviceIdType.MESH


def exchange(value, mask):
    columns = lax.axis_size("exp")
    return lax.ppermute(value, "exp", [(i, i ^ mask) for i in range(columns)])


def shift(value, step):
    seq_count = lax.axis_size("seq")
    return lax.ppermute(value, "seq", [(i, (i + step) % seq_count) for i in range(seq_count)])


def add_rounded(first, second):
    return (first.astype(jnp.float32) + second.astype(jnp.float32)).astype(jnp.bfloat16)


def attend_at(query_rows, key_rows, value_rows, position, length_row):
    row_count = query_rows.shape[0]
    groups = key_rows.shape[1] // HEAD_DIM
    per_group = query_rows.shape[1] // HEAD_DIM // groups
    bounds = jnp.cumsum(length_row)
    episode = jnp.sum((position[:, None] >= bounds[None, :]).astype(jnp.int32), axis=1)
    q_heads = query_rows.reshape(row_count, groups, per_group, HEAD_DIM)
    k_heads = key_rows.reshape(row_count, groups, HEAD_DIM)
    v_heads = value_rows.reshape(row_count, groups, HEAD_DIM)
    scores = jnp.einsum(
        "tgpd,ugd->gptu", q_heads, k_heads, preferred_element_type=jnp.float32
    ) / math.sqrt(HEAD_DIM)
    allowed = (episode[:, None] == episode[None, :]) & (position[None, :] <= position[:, None])
    scores = jnp.where(allowed, scores, -jnp.inf)
    row_maximum = jnp.max(scores, axis=-1, keepdims=True)
    weights = jnp.exp(scores - row_maximum)
    probability = (weights / jnp.sum(weights, axis=-1, keepdims=True)).astype(jnp.bfloat16)
    mixed = jnp.einsum("gptu,ugd->tgpd", probability, v_heads, preferred_element_type=jnp.float32)
    return mixed.astype(jnp.bfloat16).reshape(row_count, groups * per_group * HEAD_DIM)


def project(mixed, out_weight, token_count):
    seq_count = lax.axis_size("seq")
    columns = lax.axis_size("exp")
    width = out_weight.shape[1] // 2
    own = (out_weight[:, :width], out_weight[:, width:])
    pieces = {}
    for half, (first, second) in enumerate(((X_BIT, Y_BIT), (Y_BIT, X_BIT))):
        pieces[half, 0] = own[half]
        pieces[half, first] = exchange(own[half], first)
        pieces[half, second] = exchange(own[half], second)
        pieces[half, first | second] = exchange(pieces[half, first], second)
    for half, m in list(pieces):
        pieces[half, m | CORE] = exchange(pieces[half, m], CORE)
    groups = (
        [(h, m) for h in range(2) for m in (0, 1)],
        [(0, X_BIT), (0, X_BIT | 1), (1, Y_BIT), (1, Y_BIT | 1)],
        [(0, Y_BIT), (0, Y_BIT | 1), (1, X_BIT), (1, X_BIT | 1)],
        [(h, m) for h in range(2) for m in (6, 7)],
    )
    reduced = {}
    for names in groups:
        weight = jnp.concatenate([pieces[name] for name in names], axis=1)
        part = jnp.dot(mixed, weight, preferred_element_type=jnp.float32).astype(jnp.bfloat16)
        total = part[:token_count].astype(jnp.float32)
        for k in range(1, seq_count):
            total = total + shift(part[k * token_count : (k + 1) * token_count], -k).astype(
                jnp.float32
            )
        for place, name in enumerate(names):
            reduced[name] = total[:, place * width : (place + 1) * width]
    halves = [jnp.stack([reduced[h, m] for m in range(columns)]) for h in range(2)]
    here = lax.axis_index("exp")
    in_order = []
    for c in range(columns):
        for h in range(2):
            in_order.append(lax.dynamic_index_in_dim(halves[h], here ^ c, 0, keepdims=False))
    return jnp.concatenate(in_order, axis=1)


class Place:
    def __init__(self):
        self.z, self.e = lax.axis_index("seq"), lax.axis_index("exp")
        self.core = lax.rem(self.e, 2)
        x, y = lax.rem(lax.div(self.e, 2), 2), lax.div(self.e, 4)
        half = lax.div(self.z, 2)
        self.turn, self.flip = half, 3
        self.mid = self.z + half * (3 - 2 * self.z)
        self.to_x = (self.z, self.e + 2 - 4 * x)
        self.to_y = (self.z, self.e + 4 - 8 * y)
        self.to_core = (self.z, self.e + 1 - 2 * self.core)
        self.near = (self.line(1 - self.mid), self.e)
        self.far = (self.line(2), self.e)
        self.order = [self.line(o) for o in (self.mid, 1 - self.mid, 2, 3)]
        self.own, self.by_x = y * 2 + x, y * 2 + 1 - x
        self.by_y, self.across = (1 - y) * 2 + x, (1 - y) * 2 + 1 - x

    def line(self, place):
        return place + self.turn * (3 - 2 * place)


def experts_kernel(
    chunks,
    size,
    rows_ref,
    hidden_ref,
    gate_hbm,
    up_hbm,
    down_hbm,
    out_ref,
    held,
    from_core,
    from_plane,
    from_line,
    w_gate,
    w_up,
    w_down,
    activated,
    load_sem,
    own_sem,
    row_send,
    row_recv,
    core_send,
    core_recv,
    plane_send,
    plane_recv,
    line_send,
    line_recv,
):
    here = Place()
    mid, core = here.mid, here.core
    width = hidden_ref.shape[1]
    units = w_gate.shape[1]
    side = 16 * size

    barrier = pltpu.get_barrier_semaphore()
    for device in (here.to_x, here.to_y, here.to_core, here.near):
        pl.semaphore_signal(barrier, inc=1, device_id=device, device_id_type=MESH)

    @pl.when(mid == 1)
    def _():
        pl.semaphore_signal(barrier, inc=1, device_id=here.far, device_id_type=MESH)

    loads = [
        pltpu.make_async_copy(source, target, load_sem.at[n])
        for n, (source, target) in enumerate(((gate_hbm, w_gate), (up_hbm, w_up), (down_hbm, w_down)))
    ]

    def slot(which, i, quarter):
        return which * 16 + here.order[i] * 4 + quarter

    own_loads = [
        pltpu.make_async_copy(
            rows_ref.at[pl.ds(k * size, size)],
            held.at[k, pl.ds(pl.multiple_of(slot(core, 0, here.own) * size, size), size)],
            own_sem.at[k],
        )
        for k in range(chunks)
    ]
    for copy in own_loads + loads:
        copy.start()
    for copy in own_loads:
        copy.wait()
    pl.semaphore_wait(barrier, 4 + mid)

    def row_copy(k, which, n, device):
        block = held.at[k, pl.ds(pl.multiple_of(which * size, size), size)]
        return pltpu.make_async_remote_copy(
            src_ref=block,
            dst_ref=block,
            send_sem=row_send.at[k, n],
            recv_sem=row_recv.at[k, which],
            device_id=device,
            device_id_type=MESH,
        )

    def send_own(k):
        s = slot(core, 0, here.own)
        row_copy(k, s, 0, here.near).start()

        @pl.when(mid == 1)
        def _():
            row_copy(k, s, 1, here.far).start()

        row_copy(k, s, 5, here.to_x).start()
        row_copy(k, s, 11, here.to_y).start()
        row_copy(k, s, 17, here.to_core).start()

    def along_line(k, i):
        s = slot(core, i, here.own)
        row_copy(k, s, 0, here.near).wait_recv()

        @pl.when(mid == 1)
        def _():
            row_copy(k, s, 1 + i, here.far if i == 1 else here.near).start()

        row_copy(k, s, 5 + i, here.to_x).start()
        row_copy(k, s, 11 + i, here.to_y).start()
        row_copy(k, s, 17 + i, here.to_core).start()

    def beside(k, i):
        s = slot(core, i, here.by_x)
        row_copy(k, s, 0, here.to_x).wait_recv()
        if i % 2 == 0:
            row_copy(k, s, 15 + i // 2, here.to_y).start()
        row_copy(k, s, 21 + i, here.to_core).start()
        s = slot(core, i, here.by_y)
        row_copy(k, s, 0, here.to_y).wait_recv()
        if i % 2 == 1:
            row_copy(k, s, 9 + i // 2, here.to_x).start()
        row_copy(k, s, 25 + i, here.to_core).start()

    def across(k, i):
        s = slot(core, i, here.across)
        row_copy(k, s, 0, here.to_x).wait_recv()
        row_copy(k, s, 29 + i, here.to_core).start()

    def all_rows(k):
        @pl.loop(0, 16)
        def _(n):
            row_copy(k, (1 - core) * 16 + n, 0, here.to_core).wait_recv()

    def rows_sent(k):
        @pl.loop(5, 33)
        def _(n):
            row_copy(k, 0, n, here.to_core).wait_send()

        row_copy(k, 0, 0, here.near).wait_send()

        @pl.when(mid == 1)
        def _():
            for n in range(1, 5):
                row_copy(k, 0, n, here.near).wait_send()

    lane = here.e * EXP_COL + lax.div(here.z, 2)

    def activate(k, part, tile):
        rows = pl.ds(part * side, side)
        columns = pl.ds(tile * 256, 256)
        tokens = held[k, rows, pl.ds(0, width)]
        gates = held[k, rows, pl.ds(width, 128)].astype(jnp.float32)
        lanes = lax.broadcasted_iota(jnp.int32, gates.shape, 1)
        scale = jnp.sum(jnp.where(lanes == lane, gates, 0.0), axis=1, keepdims=True)
        gate = jnp.dot(tokens, w_gate[:, columns], preferred_element_type=jnp.float32)
        up = jnp.dot(tokens, w_up[:, columns], preferred_element_type=jnp.float32)
        value = gate / (1.0 + jnp.exp(-gate)) * up * scale
        activated[rows, columns] = value.astype(jnp.bfloat16)

    def lower(k, which):
        rows = pl.ds(pl.multiple_of(which * side, side), side)

        @pl.loop(0, width // 512)
        def _(tile):
            columns = pl.ds(pl.multiple_of(tile * 512, 512), 512)
            part = jnp.dot(activated[rows, :], w_down[:, columns], preferred_element_type=jnp.float32)
            held[k, rows, columns] = part.astype(jnp.bfloat16)

    def core_copy(k, i):
        def group(which):
            return pl.ds(pl.multiple_of((which * 16 + here.order[i] * 4) * size, 4 * size), 4 * size)

        return pltpu.make_async_remote_copy(
            src_ref=held.at[k, group(1 - core), pl.ds(0, width)],
            dst_ref=from_core.at[k, i],
            send_sem=core_send.at[k, i],
            recv_sem=core_recv.at[k, i],
            device_id=here.to_core,
            device_id_type=MESH,
        )

    def mine(k, i, quarter):
        return held.at[
            k, pl.ds(pl.multiple_of(slot(core, i, quarter) * size, size), size), pl.ds(0, width)
        ]

    def both(k, i, quarter):
        other = from_core[k, i, pl.ds(pl.multiple_of(quarter * size, size), size), :]
        return mine(k, i, quarter)[...].astype(jnp.float32) + other.astype(jnp.float32)

    def plane_copy(k, i, kind, quarter, device):
        return pltpu.make_async_remote_copy(
            src_ref=mine(k, i, quarter),
            dst_ref=from_plane.at[k, 4 * kind + i],
            send_sem=plane_send.at[k, 4 * kind + i],
            recv_sem=plane_recv.at[k, 4 * kind + i],
            device_id=device,
            device_id_type=MESH,
        )

    def links(i):
        if i % 2 == 0:
            return here.to_y, here.to_x, here.by_y, here.by_x
        return here.to_x, here.to_y, here.by_x, here.by_y

    def leave(k, i):
        first, _, direct, _ = links(i)
        core_copy(k, i).wait_recv()
        mine(k, i, here.across)[...] = both(k, i, here.across).astype(jnp.bfloat16)
        plane_copy(k, i, 0, here.across, first).start()
        mine(k, i, direct)[...] = both(k, i, direct).astype(jnp.bfloat16)
        plane_copy(k, i, 1, direct, first).start()

    def pass_on(k, i):
        first, second, _, onward = links(i)
        plane_copy(k, i, 0, onward, first).wait_recv()
        total = both(k, i, onward) + from_plane[k, i].astype(jnp.float32)
        mine(k, i, onward)[...] = total.astype(jnp.bfloat16)
        plane_copy(k, i, 2, onward, second).start()

    def line_copy(k, i, n, to, device):
        return pltpu.make_async_remote_copy(
            src_ref=mine(k, i, here.own),
            dst_ref=from_line.at[k, to],
            send_sem=line_send.at[k, n],
            recv_sem=line_recv.at[k, to],
            device_id=device,
            device_id_type=MESH,
        )

    def line_got(k, to):
        line_copy(k, 0, 0, to, here.near).wait_recv()
        return from_line[k, to].astype(jnp.float32)

    def line_sum(k, i):
        first, second, _, _ = links(i)
        plane_copy(k, i, 1, here.own, first).wait_recv()
        plane_copy(k, i, 2, here.own, second).wait_recv()
        total = both(k, i, here.own) + from_plane[k, 4 + i].astype(jnp.float32)
        return total + from_plane[k, 8 + i].astype(jnp.float32)

    def finish(k, i):
        if i == 0:
            tokens = pl.ds(pl.multiple_of(k * size, size), size)
            total = hidden_ref[tokens, :] + line_sum(k, 0)

            @pl.when(mid == 0)
            def _():
                out_ref[tokens, :] = (total + line_got(k, 0)).astype(jnp.bfloat16)

            @pl.when(mid == 1)
            def _():
                sum_near = total + line_got(k, 0)
                out_ref[tokens, :] = (sum_near + line_got(k, 3)).astype(jnp.bfloat16)

            return
        total = line_sum(k, i)

        @pl.when(mid == 0)
        def _():
            mine(k, i, here.own)[...] = total.astype(jnp.bfloat16)
            line_copy(k, i, i - 1, i - 1, here.near).start()

        @pl.when(mid == 1)
        def _():
            passed = total + line_got(k, (4, 1, 2)[i - 1])
            mine(k, i, here.own)[...] = passed.astype(jnp.bfloat16)
            device = here.near if i == 1 else here.far
            line_copy(k, i, i - 1, (0, 3, 4)[i - 1], device).start()

    def sums_sent(k):
        for i in range(4):
            core_copy(k, i).wait_send()
            for kind in range(3):
                plane_copy(k, i, kind, here.own, here.to_x).wait_send()
        for n in range(3):
            line_copy(k, 0, n, 0, here.near).wait_send()

    ahead = (
        [functools.partial(along_line, i=i) for i in (1,)]
        + [functools.partial(beside, i=0)]
        + [functools.partial(along_line, i=2)]
        + [functools.partial(beside, i=1), functools.partial(across, i=0)]
        + [functools.partial(along_line, i=3)]
        + [functools.partial(beside, i=2), functools.partial(across, i=1)]
        + [functools.partial(beside, i=3), functools.partial(across, i=2), functools.partial(across, i=3)]
    )
    behind = [functools.partial(leave, i=i) for i in (3, 2)]
    behind += [functools.partial(pass_on, i=3), functools.partial(leave, i=1)]
    behind += [functools.partial(pass_on, i=2), functools.partial(leave, i=0)]
    behind += [functools.partial(finish, i=3), functools.partial(pass_on, i=1)]
    behind += [functools.partial(finish, i=2), functools.partial(pass_on, i=0)]
    behind += [functools.partial(finish, i=1), functools.partial(finish, i=0)]

    send_own(0)
    for event in ahead:
        event(0)
    for copy in loads:
        copy.wait()

    work = [("up", part, tile) for part in range(2) for tile in range(units // 256)]
    work += [("down", None, None), ("down", None, None)]

    @pl.loop(0, chunks + 1)
    def _(k):
        more, back, now = k + 1 < chunks, k >= 1, k < chunks
        later, before = lax.rem(k + 1, chunks), lax.rem(k + chunks - 1, chunks)

        @pl.when(now)
        def _():
            all_rows(k)

        @pl.when(more)
        def _():
            send_own(later)

        steps = len(work)
        for n, (kind, part, tile) in enumerate(work):
            mine_ahead = ahead[n * len(ahead) // steps : (n + 1) * len(ahead) // steps]
            mine_behind = behind[n * len(behind) // steps : (n + 1) * len(behind) // steps]

            @pl.when(back)
            def _():
                for event in mine_behind:
                    event(before)

            @pl.when(more)
            def _():
                for event in mine_ahead:
                    event(later)

            @pl.when(now)
            def _():
                if kind == "up":
                    activate(k, part, tile)
                elif n == steps - 2:
                    rows_sent(k)
                    lower(k, 1 - core)
                    for i in (3, 2, 1, 0):
                        core_copy(k, i).start()
                else:
                    lower(k, core)

    @pl.loop(0, chunks)
    def _(k):
        sums_sent(k)


def experts(rows, hidden, w_gate, w_up, w_down):
    tokens, width = hidden.shape
    size = ROWS
    chunks = tokens // size
    wide = rows.shape[1]
    units = w_gate.shape[1]
    anywhere = pl.BlockSpec(memory_space=pl.ANY)
    inside = pl.BlockSpec(memory_space=pltpu.VMEM)
    dma = pltpu.SemaphoreType.DMA
    half = jnp.bfloat16
    return pl.pallas_call(
        functools.partial(experts_kernel, chunks, size),
        out_shape=jax.ShapeDtypeStruct((tokens, width), half),
        in_specs=[anywhere, inside, anywhere, anywhere, anywhere],
        out_specs=inside,
        scratch_shapes=[
            pltpu.VMEM((chunks, 32 * size, wide), half),
            pltpu.VMEM((chunks, 4, 4 * size, width), half),
            pltpu.VMEM((chunks, 12, size, width), half),
            pltpu.VMEM((chunks, 5, size, width), half),
            pltpu.VMEM(w_gate.shape, half),
            pltpu.VMEM(w_up.shape, half),
            pltpu.VMEM(w_down.shape, half),
            pltpu.VMEM((32 * size, units), half),
            dma((3,)),
            dma((chunks,)),
            dma((chunks, 33)),
            dma((chunks, 32)),
            dma((chunks, 4)),
            dma((chunks, 4)),
            dma((chunks, 12)),
            dma((chunks, 12)),
            dma((chunks, 3)),
            dma((chunks, 5)),
        ],
        compiler_params=pltpu.CompilerParams(
            collective_id=0, has_side_effects=True, vmem_limit_bytes=66_000_000
        ),
    )(rows, hidden, w_gate, w_up, w_down)


def local_dense(
    queries,
    key_heads,
    value_heads,
    residual,
    lengths,
    routes,
    gate_weights,
    out_weight,
    norm_gain,
    w_gate,
    w_up,
    w_down,
):
    seq_count = lax.axis_size("seq")
    columns = lax.axis_size("exp")
    token_count = residual.shape[1]
    place = lax.axis_index("seq")

    def heads_of(k):
        owner = lax.rem(place + k, seq_count)
        parts = []
        for whole in (queries[0], key_heads[0], value_heads[0]):
            width = whole.shape[1] // seq_count
            parts.append(lax.dynamic_slice_in_dim(whole, owner * width, width, axis=1))
        return jnp.concatenate(parts, axis=1)

    arrived = [heads_of(0)] + [shift(heads_of(k), k) for k in range(1, seq_count)]
    rows = jnp.concatenate(arrived, axis=0)
    q_width = queries.shape[2] // seq_count
    k_width = key_heads.shape[2] // seq_count
    position = jnp.concatenate(
        [
            lax.rem(place - k + seq_count, seq_count) * token_count
            + jnp.arange(token_count, dtype=jnp.int32)
            for k in range(seq_count)
        ]
    )
    mixed = attend_at(
        rows[:, :q_width],
        rows[:, q_width : q_width + k_width],
        rows[:, q_width + k_width :],
        position,
        lengths[0],
    )

    routed = routes[0]
    node_count = routed.shape[1]
    on_node = routed[:, :, None] == jnp.arange(columns, dtype=jnp.int32)[None, None, :]
    gate_pair = gate_weights[0].reshape(token_count, node_count, EXP_COL).astype(jnp.float32)
    node_gate = jnp.sum(jnp.where(on_node[:, :, :, None], gate_pair[:, :, None, :], 0.0), axis=1)
    node_gate = node_gate.astype(jnp.bfloat16).reshape(token_count, columns * EXP_COL)
    node_gate = jnp.pad(node_gate, ((0, 0), (0, 128 - columns * EXP_COL)))

    hidden = residual[0].astype(jnp.float32) + project(mixed, out_weight, token_count)
    inverse = lax.rsqrt(jnp.mean(hidden * hidden, axis=1, keepdims=True) + epsilon)
    normalized_rows = (hidden * inverse * norm_gain[None, :]).astype(jnp.bfloat16)
    rows = jnp.concatenate([normalized_rows, node_gate], axis=1)
    return experts(rows, hidden, w_gate[0, 0], w_up[0, 0], w_down[0, 0])[None]


def solution(mesh):
    cube = (CORE | X_BIT | Y_BIT) + 1
    dense = mesh.shape["exp"] == cube and mesh.shape["seq"] == 4
    return jax.shard_map(
        local_dense if dense else local_routed,
        mesh=mesh,
        in_specs=(
            P("exp", "seq", None),
            P("exp", "seq", None),
            P("exp", "seq", None),
            P("exp", "seq", None),
            P("exp", None),
            P("exp", "seq", None),
            P("exp", "seq", None),
            P("seq", "exp"),
            P(),
            P("exp", "seq", None, None),
            P("exp", "seq", None, None),
            P("exp", "seq", None, None),
        ),
        out_specs=P("exp", "seq", None),
        check_vma=False,
    )
```

```python
import functools
import math

import jax
import jax.numpy as jnp
from jax import lax
from jax.experimental import pallas as pl
from jax.experimental.pallas import tpu as pltpu
from jax.sharding import PartitionSpec as P

HEAD_DIM = 128
EXP_COL = 2


epsilon = 1e-06


def episode_ids(length_row, position_count):
    bounds = jnp.cumsum(length_row)
    position = jnp.arange(position_count, dtype=jnp.int32)
    return jnp.sum((position[:, None] >= bounds[None, :]).astype(jnp.int32), axis=1)


def attend(query_rows, key_rows, value_rows, episode):
    row_count = query_rows.shape[0]
    groups = key_rows.shape[1] // HEAD_DIM
    per_group = query_rows.shape[1] // HEAD_DIM // groups
    q_heads = query_rows.reshape(row_count, groups, per_group, HEAD_DIM)
    k_heads = key_rows.reshape(row_count, groups, HEAD_DIM)
    v_heads = value_rows.reshape(row_count, groups, HEAD_DIM)
    scores = jnp.einsum(
        "tgpd,ugd->gptu", q_heads, k_heads, preferred_element_type=jnp.float32
    ) / math.sqrt(HEAD_DIM)
    position = jnp.arange(row_count, dtype=jnp.int32)
    allowed = (episode[:, None] == episode[None, :]) & (position[None, :] <= position[:, None])
    scores = jnp.where(allowed, scores, -jnp.inf)
    row_maximum = jnp.max(scores, axis=-1, keepdims=True)
    weights = jnp.exp(scores - row_maximum)
    probability = (weights / jnp.sum(weights, axis=-1, keepdims=True)).astype(jnp.bfloat16)
    mixed = jnp.einsum("gptu,ugd->tgpd", probability, v_heads, preferred_element_type=jnp.float32)
    return mixed.astype(jnp.bfloat16).reshape(row_count, groups * per_group * HEAD_DIM)


def local_routed(
    queries,
    key_heads,
    value_heads,
    residual,
    lengths,
    routes,
    gate_weights,
    out_weight,
    norm_gain,
    w_gate,
    w_up,
    w_down,
):
    seq_count = lax.axis_size("seq")
    columns = lax.axis_size("exp")
    token_count = residual.shape[1]
    model_width = residual.shape[2]
    whole_q, whole_k, whole_v = (
        lax.all_to_all(queries[0], "seq", split_axis=1, concat_axis=0, tiled=True),
        lax.all_to_all(key_heads[0], "seq", split_axis=1, concat_axis=0, tiled=True),
        lax.all_to_all(value_heads[0], "seq", split_axis=1, concat_axis=0, tiled=True),
    )
    episode = episode_ids(lengths[0], whole_q.shape[0])
    mixed = attend(whole_q, whole_k, whole_v, episode)
    head_partial = jnp.dot(
        mixed,
        lax.all_gather(out_weight, "exp", axis=1, tiled=True),
        preferred_element_type=jnp.float32,
    )
    projected = lax.psum_scatter(
        head_partial.astype(jnp.bfloat16), "seq", scatter_dimension=0, tiled=True
    ).astype(jnp.float32)
    hidden = residual[0].astype(jnp.float32) + projected
    inverse = lax.rsqrt(jnp.mean(hidden * hidden, axis=1, keepdims=True) + epsilon)
    normalized_rows = (hidden * inverse * norm_gain[None, :]).astype(jnp.bfloat16)
    routed = routes[0]
    node_count = routed.shape[1]
    capacity = max(2, 5 * token_count * node_count // (4 * columns))
    on_node = routed[:, :, None] == jnp.arange(columns, dtype=jnp.int32)[None, None, :]
    member = jnp.sum(on_node.astype(jnp.int32), axis=1)
    before = jnp.cumsum(member, axis=0) - member
    slot_lookup_index = (
        before[:, :, None] == jnp.arange(capacity, dtype=jnp.int32)[None, None, :]
    ) & (member[:, :, None] > 0)
    slot_flag_mask = slot_lookup_index.astype(jnp.bfloat16)
    outbound = jnp.einsum(
        "roj,rm->ojm", slot_flag_mask, normalized_rows, preferred_element_type=jnp.float32
    ).astype(jnp.bfloat16)
    gate_pair = gate_weights[0].reshape(token_count, node_count, EXP_COL).astype(jnp.float32)
    node_route_gate = jnp.einsum(
        "tnc,tne->tce", on_node.astype(jnp.float32), gate_pair, precision=lax.Precision.HIGHEST
    )
    slot_gate = jnp.einsum(
        "qnr,qny->nry",
        slot_lookup_index.astype(jnp.float32),
        node_route_gate,
        precision=lax.Precision.HIGHEST,
    ).astype(jnp.bfloat16)
    rows_in, gate_in = (
        lax.all_to_all(outbound, "exp", split_axis=0, concat_axis=0, tiled=True),
        lax.all_to_all(slot_gate, "exp", split_axis=0, concat_axis=0, tiled=True),
    )
    rows_all, gate_all = (
        lax.all_gather(rows_in, "seq", axis=0, tiled=True),
        lax.all_gather(gate_in, "seq", axis=0, tiled=True),
    )
    halves = seq_count // EXP_COL
    expert_pick = lax.axis_index("seq") // halves
    flat_rows = rows_all.reshape(-1, model_width)
    flat_gate = lax.dynamic_index_in_dim(
        gate_all.reshape(-1, EXP_COL), expert_pick, axis=1, keepdims=False
    )
    gate_block = w_gate[0, 0]
    up_block = w_up[0, 0]
    down_block = w_down[0, 0]
    gate_proj = jnp.dot(flat_rows, gate_block, preferred_element_type=jnp.float32)
    up_proj = jnp.dot(flat_rows, up_block, preferred_element_type=jnp.float32)
    activated = (jax.nn.silu(gate_proj) * up_proj).astype(jnp.bfloat16)
    partial_value = jnp.dot(activated, down_block, preferred_element_type=jnp.float32).astype(
        jnp.bfloat16
    )
    partial_value = lax.optimization_barrier(partial_value)
    node_sum = lax.psum_scatter(
        (partial_value.astype(jnp.float32) * flat_gate.astype(jnp.float32)[:, None]).astype(
            jnp.bfloat16
        ),
        "seq",
        scatter_dimension=0,
        tiled=True,
    )
    gathered_output = lax.all_to_all(
        node_sum.reshape(columns, capacity, model_width),
        "exp",
        split_axis=0,
        concat_axis=0,
        tiled=True,
    )
    mixture_expert_total = jnp.einsum(
        "gyr,yre->ge", slot_flag_mask, gathered_output, preferred_element_type=jnp.float32
    )
    return (hidden + mixture_expert_total).astype(jnp.bfloat16)[None]

CORE, X_BIT, Y_BIT = 1, 2, 4
ROWS = 16
CHUNKS = 4
MESH = pl.DeviceIdType.MESH


def exchange(value, mask):
    columns = lax.axis_size("exp")
    return lax.ppermute(value, "exp", [(i, i ^ mask) for i in range(columns)])


def shift(value, step):
    seq_count = lax.axis_size("seq")
    return lax.ppermute(value, "seq", [(i, (i + step) % seq_count) for i in range(seq_count)])


def add_rounded(first, second):
    return (first.astype(jnp.float32) + second.astype(jnp.float32)).astype(jnp.bfloat16)


def attend_at(query_rows, key_rows, value_rows, position, length_row):
    row_count = query_rows.shape[0]
    groups = key_rows.shape[1] // HEAD_DIM
    per_group = query_rows.shape[1] // HEAD_DIM // groups
    bounds = jnp.cumsum(length_row)
    episode = jnp.sum((position[:, None] >= bounds[None, :]).astype(jnp.int32), axis=1)
    q_heads = query_rows.reshape(row_count, groups, per_group, HEAD_DIM)
    k_heads = key_rows.reshape(row_count, groups, HEAD_DIM)
    v_heads = value_rows.reshape(row_count, groups, HEAD_DIM)
    scores = jnp.einsum(
        "tgpd,ugd->gptu", q_heads, k_heads, preferred_element_type=jnp.float32
    ) / math.sqrt(HEAD_DIM)
    allowed = (episode[:, None] == episode[None, :]) & (position[None, :] <= position[:, None])
    scores = jnp.where(allowed, scores, -jnp.inf)
    row_maximum = jnp.max(scores, axis=-1, keepdims=True)
    weights = jnp.exp(scores - row_maximum)
    probability = (weights / jnp.sum(weights, axis=-1, keepdims=True)).astype(jnp.bfloat16)
    mixed = jnp.einsum("gptu,ugd->tgpd", probability, v_heads, preferred_element_type=jnp.float32)
    return mixed.astype(jnp.bfloat16).reshape(row_count, groups * per_group * HEAD_DIM)


def project(mixed, out_weight, token_count):
    seq_count = lax.axis_size("seq")
    columns = lax.axis_size("exp")
    width = out_weight.shape[1] // 2
    own = (out_weight[:, :width], out_weight[:, width:])
    pieces = {}
    for half, (first, second) in enumerate(((X_BIT, Y_BIT), (Y_BIT, X_BIT))):
        pieces[half, 0] = own[half]
        pieces[half, first] = exchange(own[half], first)
        pieces[half, second] = exchange(own[half], second)
        pieces[half, first | second] = exchange(pieces[half, first], second)
    for half, m in list(pieces):
        pieces[half, m | CORE] = exchange(pieces[half, m], CORE)
    groups = (
        [(h, m) for h in range(2) for m in (0, 1)],
        [(0, X_BIT), (0, X_BIT | 1), (1, Y_BIT), (1, Y_BIT | 1)],
        [(0, Y_BIT), (0, Y_BIT | 1), (1, X_BIT), (1, X_BIT | 1)],
        [(h, m) for h in range(2) for m in (6, 7)],
    )
    reduced = {}
    for names in groups:
        weight = jnp.concatenate([pieces[name] for name in names], axis=1)
        part = jnp.dot(mixed, weight, preferred_element_type=jnp.float32).astype(jnp.bfloat16)
        total = part[:token_count].astype(jnp.float32)
        for k in range(1, seq_count):
            total = total + shift(part[k * token_count : (k + 1) * token_count], -k).astype(
                jnp.float32
            )
        for place, name in enumerate(names):
            reduced[name] = total[:, place * width : (place + 1) * width]
    halves = [jnp.stack([reduced[h, m] for m in range(columns)]) for h in range(2)]
    here = lax.axis_index("exp")
    in_order = []
    for c in range(columns):
        for h in range(2):
            in_order.append(lax.dynamic_index_in_dim(halves[h], here ^ c, 0, keepdims=False))
    return jnp.concatenate(in_order, axis=1)


SCHEDULE = (
    (
        0, 10, 20, 110, 100, 200, 120, 300, 103, 102, 101, 203, 202, 201, 113, 303, 30, 210, 301,
        302, 112, 400
    ),
    (111,),
    (),
    (213, 220),
    (122, 212, 211),
    (130, 123),
    (),
    (310, 900, 311, 313),
    (121, 502, 312, 131),
    (),
    (223,),
    (410, 222),
    (221, 503),
    (323, 230),
    (),
    (132, 910),
    (603, 231, 321, 133, 322, 501, 320),
    (513, 510, 420, 232),
    (512,),
    (602,),
    (233, 703),
    (),
    (),
    (613, 920, 612),
    (610, 331, 332, 523, 601, 521, 511, 330, 333, 522, 713, 520, 430),
    (712,),
    (),
    (),
    (623,),
    (),
    (702, 621, 622, 701),
    (930, 723, 611),
    (
        532, 533, 721, 722, 633, 632, 530, 711, 531, 620, 733, 810, 732, 630, 631, 500, 731, 600,
        820, 830, 800
    ),
)


class Place:
    def __init__(self):
        self.z, self.e = lax.axis_index("seq"), lax.axis_index("exp")
        self.core = lax.rem(self.e, 2)
        x, y = lax.rem(lax.div(self.e, 2), 2), lax.div(self.e, 4)
        half = lax.div(self.z, 2)
        self.turn = half
        self.mid = self.z + half * (3 - 2 * self.z)
        self.to_x = (self.z, self.e + 2 - 4 * x)
        self.to_y = (self.z, self.e + 4 - 8 * y)
        self.to_core = (self.z, self.e + 1 - 2 * self.core)
        self.order = [self.line(o) for o in (self.mid, 1 - self.mid, 2, 3)]
        self.peers = [(place, self.e) for place in self.order[1:]]
        self.own, self.by_x = y * 2 + x, y * 2 + 1 - x
        self.by_y, self.across = (1 - y) * 2 + x, (1 - y) * 2 + 1 - x

    def line(self, place):
        return place + self.turn * (3 - 2 * place)


def experts_kernel(
    chunks,
    size,
    lane_count,
    rows_ref,
    hidden_ref,
    gate_hbm,
    up_hbm,
    down_hbm,
    out_ref,
    held,
    from_core,
    from_plane,
    from_line,
    w_gate,
    w_up,
    w_down,
    activated,
    load_sem,
    own_sem,
    row_send,
    row_recv,
    core_send,
    core_recv,
    plane_send,
    plane_recv,
    line_send,
    line_recv,
):
    here = Place()
    core = here.core
    width = hidden_ref.shape[1]
    units = w_gate.shape[1]
    side = 16 * size

    barrier = pltpu.get_barrier_semaphore()
    for device in (here.to_x, here.to_y, here.to_core, *here.peers):
        pl.semaphore_signal(barrier, inc=1, device_id=device, device_id_type=MESH)

    loads = [
        pltpu.make_async_copy(source, target, load_sem.at[n])
        for n, (source, target) in enumerate(((gate_hbm, w_gate), (up_hbm, w_up), (down_hbm, w_down)))
    ]

    def slot(which, i, quarter):
        return which * 16 + here.order[i] * 4 + quarter

    def columns_of(k):
        return pl.ds(0, held.shape[2] if k == 0 else width)

    own_loads = [
        pltpu.make_async_copy(
            rows_ref.at[pl.ds(k * size, size), columns_of(k)],
            held.at[
                k,
                pl.ds(pl.multiple_of(slot(core, 0, here.own) * size, size), size),
                columns_of(k),
            ],
            own_sem.at[k],
        )
        for k in range(chunks)
    ]
    for copy in own_loads + loads:
        copy.start()
    for copy in own_loads:
        copy.wait()
    pl.semaphore_wait(barrier, 6)

    def row_copy(k, which, n, device):
        block = held.at[k, pl.ds(pl.multiple_of(which * size, size), size), columns_of(k)]
        return pltpu.make_async_remote_copy(
            src_ref=block,
            dst_ref=block,
            send_sem=row_send.at[k, n],
            recv_sem=row_recv.at[k, which],
            device_id=device,
            device_id_type=MESH,
        )

    def send_peers(k):
        for n, device in enumerate(here.peers):
            row_copy(k, slot(core, 0, here.own), n, device).start()

    def along_line(k, i):
        s = slot(core, i, here.own)
        if i > 0:
            row_copy(k, s, 0, here.peers[0]).wait_recv()
        row_copy(k, s, 3 + i, here.to_x).start()
        row_copy(k, s, 9 + i, here.to_y).start()
        row_copy(k, s, 15 + i, here.to_core).start()

    def beside(k, i):
        s = slot(core, i, here.by_x)
        row_copy(k, s, 0, here.to_x).wait_recv()
        if i % 2 == 0:
            row_copy(k, s, 13 + i // 2, here.to_y).start()
        row_copy(k, s, 19 + i, here.to_core).start()
        s = slot(core, i, here.by_y)
        row_copy(k, s, 0, here.to_y).wait_recv()
        if i % 2 == 1:
            row_copy(k, s, 7 + i // 2, here.to_x).start()
        row_copy(k, s, 23 + i, here.to_core).start()

    def across(k, i):
        s = slot(core, i, here.across)
        row_copy(k, s, 0, here.to_x).wait_recv()
        row_copy(k, s, 27 + i, here.to_core).start()

    def all_rows(k):
        @pl.loop(0, 16)
        def _(n):
            row_copy(k, (1 - core) * 16 + n, 0, here.to_core).wait_recv()

    def rows_sent(k):
        @pl.loop(0, 31)
        def _(n):
            row_copy(k, 0, n, here.to_core).wait_send()

    def activate(k, which, tile):
        rows = pl.ds(pl.multiple_of(which * side, side), side)
        columns = pl.ds(tile * 256, 256)
        tokens = held[k, rows, pl.ds(0, width)]
        gates = held[0, rows, pl.ds(width, 128)].astype(jnp.float32)
        lanes = lax.broadcasted_iota(jnp.int32, gates.shape, 1)
        lane = k * lane_count + here.e * EXP_COL + lax.div(here.z, 2)
        scale = jnp.sum(jnp.where(lanes == lane, gates, 0.0), axis=1, keepdims=True)
        gate = jnp.dot(tokens, w_gate[:, columns], preferred_element_type=jnp.float32)
        up = jnp.dot(tokens, w_up[:, columns], preferred_element_type=jnp.float32)
        value = gate / (1.0 + jnp.exp(-gate)) * up * scale
        activated[rows, columns] = value.astype(jnp.bfloat16)

    def lower(k, which):
        rows = pl.ds(pl.multiple_of(which * side, side), side)

        @pl.loop(0, width // 512)
        def _(tile):
            columns = pl.ds(pl.multiple_of(tile * 512, 512), 512)
            part = jnp.dot(activated[rows, :], w_down[:, columns], preferred_element_type=jnp.float32)
            held[k, rows, columns] = part.astype(jnp.bfloat16)

    def core_copy(k, i):
        def group(which):
            return pl.ds(pl.multiple_of((which * 16 + here.order[i] * 4) * size, 4 * size), 4 * size)

        return pltpu.make_async_remote_copy(
            src_ref=held.at[k, group(1 - core), pl.ds(0, width)],
            dst_ref=from_core.at[k, i],
            send_sem=core_send.at[k, i],
            recv_sem=core_recv.at[k, i],
            device_id=here.to_core,
            device_id_type=MESH,
        )

    def mine(k, i, quarter):
        return held.at[
            k, pl.ds(pl.multiple_of(slot(core, i, quarter) * size, size), size), pl.ds(0, width)
        ]

    def both(k, i, quarter):
        other = from_core[k, i, pl.ds(pl.multiple_of(quarter * size, size), size), :]
        return mine(k, i, quarter)[...].astype(jnp.float32) + other.astype(jnp.float32)

    def plane_copy(k, i, kind, quarter, device):
        return pltpu.make_async_remote_copy(
            src_ref=mine(k, i, quarter),
            dst_ref=from_plane.at[k, 4 * kind + i],
            send_sem=plane_send.at[k, 4 * kind + i],
            recv_sem=plane_recv.at[k, 4 * kind + i],
            device_id=device,
            device_id_type=MESH,
        )

    def links(i):
        if i % 2 == 0:
            return here.to_y, here.to_x, here.by_y, here.by_x
        return here.to_x, here.to_y, here.by_x, here.by_y

    def leave(k, i):
        first, _, direct, _ = links(i)
        core_copy(k, i).wait_recv()
        mine(k, i, here.across)[...] = both(k, i, here.across).astype(jnp.bfloat16)
        plane_copy(k, i, 0, here.across, first).start()
        mine(k, i, direct)[...] = both(k, i, direct).astype(jnp.bfloat16)
        plane_copy(k, i, 1, direct, first).start()

    def pass_on(k, i):
        first, second, _, onward = links(i)
        plane_copy(k, i, 0, onward, first).wait_recv()
        total = both(k, i, onward) + from_plane[k, i].astype(jnp.float32)
        mine(k, i, onward)[...] = total.astype(jnp.bfloat16)
        plane_copy(k, i, 2, onward, second).start()

    def line_copy(k, i, source):
        return pltpu.make_async_remote_copy(
            src_ref=mine(k, i, here.own),
            dst_ref=from_line.at[k, source],
            send_sem=line_send.at[k, max(i, 1) - 1],
            recv_sem=line_recv.at[k, source],
            device_id=here.peers[max(i, 1) - 1],
            device_id_type=MESH,
        )

    def line_sum(k, i):
        first, second, _, _ = links(i)
        plane_copy(k, i, 1, here.own, first).wait_recv()
        plane_copy(k, i, 2, here.own, second).wait_recv()
        total = both(k, i, here.own) + from_plane[k, 4 + i].astype(jnp.float32)
        return total + from_plane[k, 8 + i].astype(jnp.float32)

    def send_line(k, i):
        mine(k, i, here.own)[...] = line_sum(k, i).astype(jnp.bfloat16)
        line_copy(k, i, here.z).start()

    def finish(k):
        tokens = pl.ds(pl.multiple_of(k * size, size), size)
        total = hidden_ref[tokens, :] + line_sum(k, 0)
        for source in here.order[1:]:
            line_copy(k, 0, source).wait_recv()
            total = total + from_line[k, source].astype(jnp.float32)
        out_ref[tokens, :] = total.astype(jnp.bfloat16)

    def sums_sent(k):
        for i in range(4):
            core_copy(k, i).wait_send()
            for kind in range(3):
                plane_copy(k, i, kind, here.own, here.to_x).wait_send()
        for i in range(1, 4):
            line_copy(k, i, 0).wait_send()

    def send_core(k):
        for i in (3, 2, 1, 0):
            core_copy(k, i).start()

    moves = (
        lambda k, i: send_peers(k),
        along_line,
        beside,
        across,
        lambda k, i: all_rows(k),
        leave,
        pass_on,
        send_line,
        lambda k, i: finish(k),
        lambda k, i: send_core(k),
    )

    def run(events):
        for event in events:
            moves[event // 100](event // 10 % 10, event % 10)

    tiles = units // 256
    steps = 2 * tiles + 2
    run(SCHEDULE[0])
    for copy in loads:
        copy.wait()

    @pl.loop(0, chunks)
    def _(k):
        for n in range(steps):
            if n < 2 * tiles:
                activate(k, core if n < tiles else 1 - core, n % tiles)
            elif n == 2 * tiles:
                for chunk in range(chunks):
                    pl.when(k == chunk)(functools.partial(rows_sent, chunk))
                lower(k, 1 - core)
            else:
                lower(k, core)
            for chunk in range(chunks):
                events = SCHEDULE[1 + chunk * steps + n]
                if events:
                    pl.when(k == chunk)(functools.partial(run, events))

    for k in range(chunks):
        sums_sent(k)


def experts(rows, hidden, lane_count, w_gate, w_up, w_down):
    tokens, width = hidden.shape
    size = ROWS
    chunks = tokens // size
    wide = rows.shape[1]
    units = w_gate.shape[1]
    anywhere = pl.BlockSpec(memory_space=pl.ANY)
    inside = pl.BlockSpec(memory_space=pltpu.VMEM)
    dma = pltpu.SemaphoreType.DMA
    half = jnp.bfloat16
    return pl.pallas_call(
        functools.partial(experts_kernel, chunks, size, lane_count),
        out_shape=jax.ShapeDtypeStruct((tokens, width), half),
        in_specs=[anywhere, inside, anywhere, anywhere, anywhere],
        out_specs=inside,
        scratch_shapes=[
            pltpu.VMEM((chunks, 32 * size, wide), half),
            pltpu.VMEM((chunks, 4, 4 * size, width), half),
            pltpu.VMEM((chunks, 12, size, width), half),
            pltpu.VMEM((chunks, 4, size, width), half),
            pltpu.VMEM(w_gate.shape, half),
            pltpu.VMEM(w_up.shape, half),
            pltpu.VMEM(w_down.shape, half),
            pltpu.VMEM((32 * size, units), half),
            dma((3,)),
            dma((chunks,)),
            dma((chunks, 31)),
            dma((chunks, 32)),
            dma((chunks, 4)),
            dma((chunks, 4)),
            dma((chunks, 12)),
            dma((chunks, 12)),
            dma((chunks, 3)),
            dma((chunks, 4)),
        ],
        compiler_params=pltpu.CompilerParams(
            collective_id=0, has_side_effects=True, vmem_limit_bytes=66_000_000
        ),
    )(rows, hidden, w_gate, w_up, w_down)


def local_dense(
    queries,
    key_heads,
    value_heads,
    residual,
    lengths,
    routes,
    gate_weights,
    out_weight,
    norm_gain,
    w_gate,
    w_up,
    w_down,
):
    seq_count = lax.axis_size("seq")
    columns = lax.axis_size("exp")
    token_count = residual.shape[1]
    place = lax.axis_index("seq")

    def heads_of(k):
        owner = lax.rem(place + k, seq_count)
        parts = []
        for whole in (queries[0], key_heads[0], value_heads[0]):
            width = whole.shape[1] // seq_count
            parts.append(lax.dynamic_slice_in_dim(whole, owner * width, width, axis=1))
        return jnp.concatenate(parts, axis=1)

    arrived = [heads_of(0)] + [shift(heads_of(k), k) for k in range(1, seq_count)]
    rows = jnp.concatenate(arrived, axis=0)
    q_width = queries.shape[2] // seq_count
    k_width = key_heads.shape[2] // seq_count
    position = jnp.concatenate(
        [
            lax.rem(place - k + seq_count, seq_count) * token_count
            + jnp.arange(token_count, dtype=jnp.int32)
            for k in range(seq_count)
        ]
    )
    mixed = attend_at(
        rows[:, :q_width],
        rows[:, q_width : q_width + k_width],
        rows[:, q_width + k_width :],
        position,
        lengths[0],
    )

    routed = routes[0]
    node_count = routed.shape[1]
    on_node = routed[:, :, None] == jnp.arange(columns, dtype=jnp.int32)[None, None, :]
    gate_pair = gate_weights[0].reshape(token_count, node_count, EXP_COL).astype(jnp.float32)
    node_gate = jnp.sum(jnp.where(on_node[:, :, :, None], gate_pair[:, :, None, :], 0.0), axis=1)
    node_gate = node_gate.astype(jnp.bfloat16).reshape(CHUNKS, ROWS, columns * EXP_COL)
    node_gate = jnp.transpose(node_gate, (1, 0, 2)).reshape(ROWS, -1)
    node_gate = jnp.pad(node_gate, ((0, token_count - ROWS), (0, 128 - node_gate.shape[1])))

    hidden = residual[0].astype(jnp.float32) + project(mixed, out_weight, token_count)
    inverse = lax.rsqrt(jnp.mean(hidden * hidden, axis=1, keepdims=True) + epsilon)
    normalized_rows = (hidden * inverse * norm_gain[None, :]).astype(jnp.bfloat16)
    rows = jnp.concatenate([normalized_rows, node_gate], axis=1)
    weights = w_gate[0, 0], w_up[0, 0], w_down[0, 0]
    return experts(rows, hidden, columns * EXP_COL, *weights)[None]


def solution(mesh):
    cube = (CORE | X_BIT | Y_BIT) + 1
    plane = mesh.shape["exp"] == cube and mesh.shape["seq"] == 4

    def local(*arguments):
        dense = plane and arguments[3].shape[1] == CHUNKS * ROWS
        return (local_dense if dense else local_routed)(*arguments)

    return jax.shard_map(
        local,
        mesh=mesh,
        in_specs=(
            P("exp", "seq", None),
            P("exp", "seq", None),
            P("exp", "seq", None),
            P("exp", "seq", None),
            P("exp", None),
            P("exp", "seq", None),
            P("exp", "seq", None),
            P("seq", "exp"),
            P(),
            P("exp", "seq", None, None),
            P("exp", "seq", None, None),
            P("exp", "seq", None, None),
        ),
        out_specs=P("exp", "seq", None),
        check_vma=False,
    )
```

```python
import functools
import math

import jax
import jax.numpy as jnp
from jax import lax
from jax.experimental import pallas as pl
from jax.experimental.pallas import tpu as pltpu
from jax.sharding import PartitionSpec as P

HEAD_DIM = 128
EXP_COL = 2


epsilon = 1e-06


def episode_ids(length_row, position_count):
    bounds = jnp.cumsum(length_row)
    position = jnp.arange(position_count, dtype=jnp.int32)
    return jnp.sum((position[:, None] >= bounds[None, :]).astype(jnp.int32), axis=1)


def attend(query_rows, key_rows, value_rows, episode):
    row_count = query_rows.shape[0]
    groups = key_rows.shape[1] // HEAD_DIM
    per_group = query_rows.shape[1] // HEAD_DIM // groups
    q_heads = query_rows.reshape(row_count, groups, per_group, HEAD_DIM)
    k_heads = key_rows.reshape(row_count, groups, HEAD_DIM)
    v_heads = value_rows.reshape(row_count, groups, HEAD_DIM)
    scores = jnp.einsum(
        "tgpd,ugd->gptu", q_heads, k_heads, preferred_element_type=jnp.float32
    ) / math.sqrt(HEAD_DIM)
    position = jnp.arange(row_count, dtype=jnp.int32)
    allowed = (episode[:, None] == episode[None, :]) & (position[None, :] <= position[:, None])
    scores = jnp.where(allowed, scores, -jnp.inf)
    row_maximum = jnp.max(scores, axis=-1, keepdims=True)
    weights = jnp.exp(scores - row_maximum)
    probability = (weights / jnp.sum(weights, axis=-1, keepdims=True)).astype(jnp.bfloat16)
    mixed = jnp.einsum("gptu,ugd->tgpd", probability, v_heads, preferred_element_type=jnp.float32)
    return mixed.astype(jnp.bfloat16).reshape(row_count, groups * per_group * HEAD_DIM)


def local_routed(
    queries,
    key_heads,
    value_heads,
    residual,
    lengths,
    routes,
    gate_weights,
    out_weight,
    norm_gain,
    w_gate,
    w_up,
    w_down,
):
    seq_count = lax.axis_size("seq")
    columns = lax.axis_size("exp")
    token_count = residual.shape[1]
    model_width = residual.shape[2]
    whole_q, whole_k, whole_v = (
        lax.all_to_all(queries[0], "seq", split_axis=1, concat_axis=0, tiled=True),
        lax.all_to_all(key_heads[0], "seq", split_axis=1, concat_axis=0, tiled=True),
        lax.all_to_all(value_heads[0], "seq", split_axis=1, concat_axis=0, tiled=True),
    )
    episode = episode_ids(lengths[0], whole_q.shape[0])
    mixed = attend(whole_q, whole_k, whole_v, episode)
    head_partial = jnp.dot(
        mixed,
        lax.all_gather(out_weight, "exp", axis=1, tiled=True),
        preferred_element_type=jnp.float32,
    )
    projected = lax.psum_scatter(
        head_partial.astype(jnp.bfloat16), "seq", scatter_dimension=0, tiled=True
    ).astype(jnp.float32)
    hidden = residual[0].astype(jnp.float32) + projected
    inverse = lax.rsqrt(jnp.mean(hidden * hidden, axis=1, keepdims=True) + epsilon)
    normalized_rows = (hidden * inverse * norm_gain[None, :]).astype(jnp.bfloat16)
    routed = routes[0]
    node_count = routed.shape[1]
    capacity = max(2, 5 * token_count * node_count // (4 * columns))
    on_node = routed[:, :, None] == jnp.arange(columns, dtype=jnp.int32)[None, None, :]
    member = jnp.sum(on_node.astype(jnp.int32), axis=1)
    before = jnp.cumsum(member, axis=0) - member
    slot_lookup_index = (
        before[:, :, None] == jnp.arange(capacity, dtype=jnp.int32)[None, None, :]
    ) & (member[:, :, None] > 0)
    slot_flag_mask = slot_lookup_index.astype(jnp.bfloat16)
    outbound = jnp.einsum(
        "roj,rm->ojm", slot_flag_mask, normalized_rows, preferred_element_type=jnp.float32
    ).astype(jnp.bfloat16)
    gate_pair = gate_weights[0].reshape(token_count, node_count, EXP_COL).astype(jnp.float32)
    node_route_gate = jnp.einsum(
        "tnc,tne->tce", on_node.astype(jnp.float32), gate_pair, precision=lax.Precision.HIGHEST
    )
    slot_gate = jnp.einsum(
        "qnr,qny->nry",
        slot_lookup_index.astype(jnp.float32),
        node_route_gate,
        precision=lax.Precision.HIGHEST,
    ).astype(jnp.bfloat16)
    rows_in, gate_in = (
        lax.all_to_all(outbound, "exp", split_axis=0, concat_axis=0, tiled=True),
        lax.all_to_all(slot_gate, "exp", split_axis=0, concat_axis=0, tiled=True),
    )
    rows_all, gate_all = (
        lax.all_gather(rows_in, "seq", axis=0, tiled=True),
        lax.all_gather(gate_in, "seq", axis=0, tiled=True),
    )
    halves = seq_count // EXP_COL
    expert_pick = lax.axis_index("seq") // halves
    flat_rows = rows_all.reshape(-1, model_width)
    flat_gate = lax.dynamic_index_in_dim(
        gate_all.reshape(-1, EXP_COL), expert_pick, axis=1, keepdims=False
    )
    gate_block = w_gate[0, 0]
    up_block = w_up[0, 0]
    down_block = w_down[0, 0]
    gate_proj = jnp.dot(flat_rows, gate_block, preferred_element_type=jnp.float32)
    up_proj = jnp.dot(flat_rows, up_block, preferred_element_type=jnp.float32)
    activated = (jax.nn.silu(gate_proj) * up_proj).astype(jnp.bfloat16)
    partial_value = jnp.dot(activated, down_block, preferred_element_type=jnp.float32).astype(
        jnp.bfloat16
    )
    partial_value = lax.optimization_barrier(partial_value)
    node_sum = lax.psum_scatter(
        (partial_value.astype(jnp.float32) * flat_gate.astype(jnp.float32)[:, None]).astype(
            jnp.bfloat16
        ),
        "seq",
        scatter_dimension=0,
        tiled=True,
    )
    gathered_output = lax.all_to_all(
        node_sum.reshape(columns, capacity, model_width),
        "exp",
        split_axis=0,
        concat_axis=0,
        tiled=True,
    )
    mixture_expert_total = jnp.einsum(
        "gyr,yre->ge", slot_flag_mask, gathered_output, preferred_element_type=jnp.float32
    )
    return (hidden + mixture_expert_total).astype(jnp.bfloat16)[None]

ROWS = 16
CHUNKS = 4
MESH = pl.DeviceIdType.MESH


SCHEDULE = (
    (
        1000, 1010, 1100, 0, 100, 102, 1020, 101, 200, 103, 1120, 1110, 201, 10, 202, 110, 20,
        301, 300, 203, 120, 122, 111, 1030, 302, 303, 400
    ),
    (),
    (113, 210, 112, 123, 1130),
    (121,),
    (211, 30),
    (212, 213),
    (220, 222),
    (900, 132, 311, 310, 130),
    (221, 312, 131, 313),
    (),
    (),
    (500, 410, 133),
    (),
    (223, 502, 321, 322, 320),
    (503,),
    (323, 232, 910),
    (231, 513),
    (233,),
    (512, 603, 420, 511),
    (230,),
    (501,),
    (),
    (),
    (920,),
    (600, 613, 330, 522, 703, 332, 331, 602, 612, 333, 601),
    (521,),
    (713,),
    (430, 611, 510),
    (),
    (523, 712, 621),
    (622, 702),
    (930, 623),
    (
        701, 532, 711, 533, 723, 531, 722, 633, 721, 520, 632, 610, 631, 530, 733, 620, 732, 731,
        810, 630, 820, 800, 830
    ),
)


class Place:
    def __init__(self):
        self.z, self.e = lax.axis_index("seq"), lax.axis_index("exp")
        self.core = lax.rem(self.e, 2)
        x, y = lax.rem(lax.div(self.e, 2), 2), lax.div(self.e, 4)
        self.x, self.y = x, y
        half = lax.div(self.z, 2)
        self.turn = half
        self.mid = self.z + half * (3 - 2 * self.z)
        self.to_x = (self.z, self.e + 2 - 4 * x)
        self.to_y = (self.z, self.e + 4 - 8 * y)
        self.to_core = (self.z, self.e + 1 - 2 * self.core)
        self.order = [self.line(o) for o in (self.mid, 1 - self.mid, 2, 3)]
        self.peers = [(place, self.e) for place in self.order[1:]]
        self.own, self.by_x = y * 2 + x, y * 2 + 1 - x
        self.by_y, self.across = (1 - y) * 2 + x, (1 - y) * 2 + 1 - x

    def line(self, place):
        return place + self.turn * (3 - 2 * place)


def block_kernel(
    chunks,
    size,
    query_ref,
    key_ref,
    value_ref,
    residual_ref,
    length_ref,
    route_ref,
    weight_ref,
    project_ref,
    gain_ref,
    gate_hbm,
    up_hbm,
    down_hbm,
    out_ref,
    queries,
    keys,
    values,
    mixed,
    part,
    from_heads,
    from_near,
    hidden,
    held,
    from_core,
    from_plane,
    from_line,
    w_gate,
    w_up,
    w_down,
    activated,
    load_sem,
    head_send,
    head_recv,
    project_send,
    project_recv,
    part_send,
    part_recv,
    near_recv,
    row_send,
    row_recv,
    core_send,
    core_recv,
    plane_send,
    plane_recv,
    line_send,
    line_recv,
):
    here = Place()
    core = here.core
    width = hidden.shape[1]
    lane_count = lax.axis_size("exp") * EXP_COL
    tokens_here = chunks * size
    units = w_gate.shape[1]
    side = 16 * size

    barrier = pltpu.get_barrier_semaphore()
    for device in (here.to_x, here.to_y, here.to_core, *here.peers):
        pl.semaphore_signal(barrier, inc=1, device_id=device, device_id_type=MESH)

    loads = [
        pltpu.make_async_copy(source, target, load_sem.at[n])
        for n, (source, target) in enumerate(((down_hbm, w_down), (gate_hbm, w_gate), (up_hbm, w_up)))
    ]

    def remote(source, target, sent, got, device):
        return pltpu.make_async_remote_copy(
            src_ref=source,
            dst_ref=target,
            send_sem=sent,
            recv_sem=got,
            device_id=device,
            device_id_type=MESH,
        )

    def slot(which, i, quarter):
        return which * 16 + here.order[i] * 4 + quarter

    def columns_of(k):
        return pl.ds(0, held.shape[2] if k == 0 else width)

    heads = ((key_ref, keys), (value_ref, values), (query_ref, queries))

    def head_block(target, place):
        return target.at[pl.ds(pl.multiple_of(place * tokens_here, tokens_here), tokens_here)]

    def head_columns(source, target, place):
        span = target.shape[1]
        return source.at[:, pl.ds(pl.multiple_of(place * span, span), span)]

    def head_copy(n, i, source_place):
        source, target = heads[n]
        return remote(
            head_columns(source, target, here.order[i]),
            head_block(target, source_place),
            head_send.at[n, i - 1],
            head_recv.at[n, source_place],
            here.peers[i - 1],
        )

    head_loads = [
        pltpu.make_async_copy(
            head_columns(source, target, here.z), head_block(target, here.z), load_sem.at[3 + n]
        )
        for n, (source, target) in enumerate(heads)
    ]

    depth, span = project_ref.shape
    pieces = 4
    piece = depth // pieces

    def project_place(other, x, core, p):
        buffer = w_up if other else w_gate
        start = ((x * 2 + core) * pieces + p) * piece
        return buffer.at[pl.ds(pl.multiple_of(start, piece), piece), pl.ds(0, span)]

    def project_copy(source, other, x, core, p, n, device):
        return remote(
            source,
            project_place(other, x, core, p),
            project_send.at[n],
            project_recv.at[((other * 2 + x) * 2 + core) * pieces + p],
            device,
        )

    def own_piece(p):
        return project_ref.at[pl.ds(p * piece, piece)]

    own_projects = [
        pltpu.make_async_copy(
            own_piece(p), project_place(0, here.x, core, p), load_sem.at[6 + p]
        )
        for p in range(pieces)
    ]

    def got_piece(other, x, core, p):
        place = project_place(other, x, core, p)
        project_copy(place, other, x, core, p, 0, here.to_x).wait_recv()
        return place

    def project_x(p):
        place = got_piece(0, 1 - here.x, core, p)
        if p % 2 == 0:
            project_copy(place, 1, 1 - here.x, core, p, 12 + p // 2, here.to_y).start()
        project_copy(place, 0, 1 - here.x, core, p, 16 + p, here.to_core).start()

    def project_y(p):
        place = got_piece(1, here.x, core, p)
        if p % 2 == 1:
            project_copy(place, 1, here.x, core, p, 14 + p // 2, here.to_x).start()
        project_copy(place, 1, here.x, core, p, 20 + p, here.to_core).start()

    def project_across(p):
        place = got_piece(1, 1 - here.x, core, p)
        project_copy(place, 1, 1 - here.x, core, p, 24 + p, here.to_core).start()

    groups = (
        (0, here.x, here.own),
        (0, 1 - here.x, here.by_x),
        (1, here.x, here.by_y),
        (1, 1 - here.x, here.across),
    )

    def project(g):
        other, x, quarter = groups[g]
        for p in range(pieces):
            got_piece(other, x, 1 - core, p)
        buffer = w_up if other else w_gate

        @pl.loop(0, 4)
        def _(n):
            which, half = lax.div(n, 2), lax.rem(n, 2)
            rows = pl.ds(pl.multiple_of((x * 2 + which) * depth, depth), depth)
            weight = buffer[rows, pl.ds(pl.multiple_of(half * (span // 2), span // 2), span // 2)]
            total = jnp.dot(mixed[...], weight, preferred_element_type=jnp.float32)
            start = pl.multiple_of(quarter * 2 * span + n * (span // 2), span // 2)
            part[:, pl.ds(start, span // 2)] = total.astype(jnp.bfloat16)

    def part_copy(g, i, chunk, source_place, near):
        quarter = groups[g][2]
        columns = pl.ds(pl.multiple_of(quarter * 2 * span, 2 * span), 2 * span)
        count = tokens_here if chunk is None else size
        start = 0 if chunk is None else chunk * size
        n = 0 if chunk is None else 1 + (g - 1) * chunks + chunk
        rows = pl.ds(pl.multiple_of(here.order[i] * tokens_here + start, size), count)
        if near:
            target, got = from_near.at[pl.ds(start, count), columns], near_recv.at[n]
        else:
            target = from_heads.at[source_place, pl.ds(start, count), columns]
            got = part_recv.at[source_place, n]
        device = here.peers[0] if near else here.peers[i - 1]
        return remote(part.at[rows, columns], target, part_send.at[i - 1, n], got, device)

    def send_part(g, chunk=None):
        @pl.when(here.mid == 0)
        def _():
            part_copy(g, 3, chunk, here.z, True).start()

        for i in (2, 1):
            part_copy(g, i, chunk, here.z, False).start()

    def pass_part(g, chunk=None):
        quarter = groups[g][2]
        columns = pl.ds(pl.multiple_of(quarter * 2 * span, 2 * span), 2 * span)
        count = tokens_here if chunk is None else size
        start = 0 if chunk is None else chunk * size
        rows = pl.ds(pl.multiple_of(here.order[3] * tokens_here + start, size), count)

        @pl.when(here.mid == 1)
        def _():
            part_copy(g, 3, chunk, here.z, True).wait_recv()
            total = part[rows, columns].astype(jnp.float32)
            total = total + from_near[pl.ds(start, count), columns].astype(jnp.float32)
            part[rows, columns] = total.astype(jnp.bfloat16)
            part_copy(g, 3, chunk, here.z, False).start()

    def last_groups(k):
        return (1, 2, 3) if k + 1 == chunks else (3,)

    def send_last(k):
        for g in last_groups(k):
            send_part(g, k)

    def pass_last(k):
        for g in last_groups(k):
            pass_part(g, k)

    def attend():
        count = queries.shape[0]
        rows = lax.broadcasted_iota(jnp.int32, (count, count), 0)
        columns = lax.broadcasted_iota(jnp.int32, (count, count), 1)
        row_episode, column_episode = jnp.zeros_like(rows), jnp.zeros_like(rows)
        bound = 0
        for n in range(length_ref.shape[1]):
            bound = bound + length_ref[0, n]
            row_episode += (rows >= bound).astype(jnp.int32)
            column_episode += (columns >= bound).astype(jnp.int32)
        allowed = (row_episode == column_episode) & (columns <= rows)
        kept = jnp.where(allowed, 0.0, -jnp.inf)

        @pl.loop(0, queries.shape[1] // HEAD_DIM)
        def _(head):
            lanes = pl.ds(pl.multiple_of(head * HEAD_DIM, HEAD_DIM), HEAD_DIM)
            scores = lax.dot_general(
                queries[:, lanes],
                keys[...],
                (((1,), (1,)), ((), ())),
                preferred_element_type=jnp.float32,
            )
            scores = scores * (1.0 / math.sqrt(HEAD_DIM)) + kept
            weights = jnp.exp(scores - jnp.max(scores, axis=1, keepdims=True))
            share = (weights / jnp.sum(weights, axis=1, keepdims=True)).astype(jnp.bfloat16)
            value = jnp.dot(share, values[...], preferred_element_type=jnp.float32)
            mixed[:, lanes] = value.astype(jnp.bfloat16)

    def spread_gates():
        lanes = lax.broadcasted_iota(jnp.int32, (size, 128), 1)
        total = jnp.zeros((size, 128), jnp.float32)
        for k in range(chunks):
            routed = route_ref[pl.ds(k * size, size), :]
            gates = weight_ref[pl.ds(k * size, size), :].astype(jnp.float32)
            for n in range(routed.shape[1]):
                for e in range(EXP_COL):
                    lane = k * lane_count + routed[:, n : n + 1] * EXP_COL + e
                    gate = gates[:, EXP_COL * n + e : EXP_COL * n + e + 1]
                    total += jnp.where(lanes == lane, gate, 0.0)
        return total.astype(jnp.bfloat16)

    def normalize(k):
        tokens = pl.ds(k * size, size)

        def got(place):
            if k == 0:
                part_copy(0, 1, None, place, False).wait_recv()
            for g in (1, 2, 3):
                part_copy(g, 1, k, place, False).wait_recv()
            return from_heads[place, tokens, :].astype(jnp.float32)

        mine = pl.ds(pl.multiple_of(here.z * tokens_here + k * size, size), size)
        total = residual_ref[tokens, :].astype(jnp.float32) + part[mine, :].astype(jnp.float32)
        hidden[tokens, :] = total + got(here.order[1]) + got(here.order[2])

        @pl.when(here.mid == 1)
        def _():
            hidden[tokens, :] = hidden[tokens, :] + got(here.order[3])

        total = hidden[tokens, :]
        inverse = lax.rsqrt(jnp.mean(total * total, axis=1, keepdims=True) + epsilon)
        rows = pl.ds(pl.multiple_of(slot(core, 0, here.own) * size, size), size)
        held[k, rows, pl.ds(0, width)] = (total * inverse * gain_ref[...]).astype(jnp.bfloat16)

    for copy in [loads[0], *head_loads, *own_projects]:
        copy.start()
    pl.semaphore_wait(barrier, 6)
    for n in range(3):
        for i in (1, 2, 3):
            head_copy(n, i, here.z).start()
    for p in range(pieces):
        project_copy(own_piece(p), 0, here.x, core, p, p, here.to_x).start()
        project_copy(own_piece(p), 1, here.x, core, p, 4 + p, here.to_y).start()
        project_copy(own_piece(p), 0, here.x, core, p, 8 + p, here.to_core).start()
    for p in range(2):
        project_x(p)
        project_y(p)
    for n in range(3):
        head_loads[n].wait()
        for i in (1, 2, 3):
            head_copy(n, i, here.order[i]).wait_recv()
    attend()
    for copy in own_projects:
        copy.wait()
    project(0)
    send_part(0)
    for p in range(2, pieces):
        project_x(p)
        project_y(p)
    project(1)
    project(2)
    for chunk in range(chunks - 1):
        send_part(1, chunk)
        send_part(2, chunk)
    own_rows = pl.ds(pl.multiple_of(slot(core, 0, here.own) * size, size), size)
    held[0, own_rows, pl.ds(width, 128)] = spread_gates()
    pass_part(0)
    for p in range(2):
        project_across(p)
    for chunk in range(chunks - 1):
        pass_part(1, chunk)
        pass_part(2, chunk)
    for p in range(2, pieces):
        project_across(p)
    project(3)
    for n in range(28):
        project_copy(own_piece(0), 0, here.x, core, 0, n, here.to_x).wait_send()
    for copy in loads[1:]:
        copy.start()

    def row_copy(k, which, n, device):
        block = held.at[k, pl.ds(pl.multiple_of(which * size, size), size), columns_of(k)]
        return pltpu.make_async_remote_copy(
            src_ref=block,
            dst_ref=block,
            send_sem=row_send.at[k, n],
            recv_sem=row_recv.at[k, which],
            device_id=device,
            device_id_type=MESH,
        )

    def send_peers(k):
        normalize(k)
        s = slot(core, 0, here.own)
        row_copy(k, s, 0, here.peers[0]).start()
        row_copy(k, s, 1, here.peers[1]).start()

        @pl.when(here.mid == 1)
        def _():
            row_copy(k, s, 2, here.peers[2]).start()

    def along_line(k, i):
        s = slot(core, i, here.own)
        if i > 0:
            row_copy(k, s, 0, here.peers[0]).wait_recv()
        if i == 3:

            @pl.when(here.mid == 1)
            def _():
                row_copy(k, s, 31, here.peers[0]).start()

        row_copy(k, s, 3 + i, here.to_x).start()
        row_copy(k, s, 9 + i, here.to_y).start()
        row_copy(k, s, 15 + i, here.to_core).start()

    def beside(k, i):
        s = slot(core, i, here.by_x)
        row_copy(k, s, 0, here.to_x).wait_recv()
        if i % 2 == 0:
            row_copy(k, s, 13 + i // 2, here.to_y).start()
        row_copy(k, s, 19 + i, here.to_core).start()
        s = slot(core, i, here.by_y)
        row_copy(k, s, 0, here.to_y).wait_recv()
        if i % 2 == 1:
            row_copy(k, s, 7 + i // 2, here.to_x).start()
        row_copy(k, s, 23 + i, here.to_core).start()

    def across(k, i):
        s = slot(core, i, here.across)
        row_copy(k, s, 0, here.to_x).wait_recv()
        row_copy(k, s, 27 + i, here.to_core).start()

    def all_rows(k):
        @pl.loop(0, 16)
        def _(n):
            row_copy(k, (1 - core) * 16 + n, 0, here.to_core).wait_recv()

    def rows_sent(k):
        for n in (0, 1):
            row_copy(k, 0, n, here.to_core).wait_send()

        @pl.when(here.mid == 1)
        def _():
            for n in (2, 31):
                row_copy(k, 0, n, here.to_core).wait_send()

        @pl.loop(3, 31)
        def _(n):
            row_copy(k, 0, n, here.to_core).wait_send()

    def activate(k, which, tile):
        rows = pl.ds(pl.multiple_of(which * side, side), side)
        columns = pl.ds(tile * 256, 256)
        tokens = held[k, rows, pl.ds(0, width)]
        gates = held[0, rows, pl.ds(width, 128)].astype(jnp.float32)
        lanes = lax.broadcasted_iota(jnp.int32, gates.shape, 1)
        lane = k * lane_count + here.e * EXP_COL + lax.div(here.z, 2)
        scale = jnp.sum(jnp.where(lanes == lane, gates, 0.0), axis=1, keepdims=True)
        gate = jnp.dot(tokens, w_gate[:, columns], preferred_element_type=jnp.float32)
        up = jnp.dot(tokens, w_up[:, columns], preferred_element_type=jnp.float32)
        value = gate / (1.0 + jnp.exp(-gate)) * up * scale
        activated[rows, columns] = value.astype(jnp.bfloat16)

    def lower(k, which):
        rows = pl.ds(pl.multiple_of(which * side, side), side)

        @pl.loop(0, width // 512)
        def _(tile):
            columns = pl.ds(pl.multiple_of(tile * 512, 512), 512)
            part = jnp.dot(activated[rows, :], w_down[:, columns], preferred_element_type=jnp.float32)
            held[k, rows, columns] = part.astype(jnp.bfloat16)

    def core_copy(k, i):
        def group(which):
            return pl.ds(pl.multiple_of((which * 16 + here.order[i] * 4) * size, 4 * size), 4 * size)

        return pltpu.make_async_remote_copy(
            src_ref=held.at[k, group(1 - core), pl.ds(0, width)],
            dst_ref=from_core.at[k, i],
            send_sem=core_send.at[k, i],
            recv_sem=core_recv.at[k, i],
            device_id=here.to_core,
            device_id_type=MESH,
        )

    def mine(k, i, quarter):
        return held.at[
            k, pl.ds(pl.multiple_of(slot(core, i, quarter) * size, size), size), pl.ds(0, width)
        ]

    def both(k, i, quarter):
        other = from_core[k, i, pl.ds(pl.multiple_of(quarter * size, size), size), :]
        return mine(k, i, quarter)[...].astype(jnp.float32) + other.astype(jnp.float32)

    def plane_copy(k, i, kind, quarter, device):
        return pltpu.make_async_remote_copy(
            src_ref=mine(k, i, quarter),
            dst_ref=from_plane.at[k, 4 * kind + i],
            send_sem=plane_send.at[k, 4 * kind + i],
            recv_sem=plane_recv.at[k, 4 * kind + i],
            device_id=device,
            device_id_type=MESH,
        )

    def links(i):
        if i % 2 == 0:
            return here.to_y, here.to_x, here.by_y, here.by_x
        return here.to_x, here.to_y, here.by_x, here.by_y

    def leave(k, i):
        first, _, direct, _ = links(i)
        core_copy(k, i).wait_recv()
        mine(k, i, here.across)[...] = both(k, i, here.across).astype(jnp.bfloat16)
        plane_copy(k, i, 0, here.across, first).start()
        mine(k, i, direct)[...] = both(k, i, direct).astype(jnp.bfloat16)
        plane_copy(k, i, 1, direct, first).start()

    def pass_on(k, i):
        first, second, _, onward = links(i)
        plane_copy(k, i, 0, onward, first).wait_recv()
        total = both(k, i, onward) + from_plane[k, i].astype(jnp.float32)
        mine(k, i, onward)[...] = total.astype(jnp.bfloat16)
        plane_copy(k, i, 2, onward, second).start()

    def line_copy(k, i, source):
        return pltpu.make_async_remote_copy(
            src_ref=mine(k, i, here.own),
            dst_ref=from_line.at[k, source],
            send_sem=line_send.at[k, max(i, 1) - 1],
            recv_sem=line_recv.at[k, source],
            device_id=here.peers[max(i, 1) - 1],
            device_id_type=MESH,
        )

    def line_sum(k, i):
        first, second, _, _ = links(i)
        plane_copy(k, i, 1, here.own, first).wait_recv()
        plane_copy(k, i, 2, here.own, second).wait_recv()
        total = both(k, i, here.own) + from_plane[k, 4 + i].astype(jnp.float32)
        return total + from_plane[k, 8 + i].astype(jnp.float32)

    def send_line(k, i):
        mine(k, i, here.own)[...] = line_sum(k, i).astype(jnp.bfloat16)
        line_copy(k, i, here.z).start()

    def finish(k):
        tokens = pl.ds(pl.multiple_of(k * size, size), size)
        total = hidden[tokens, :] + line_sum(k, 0)
        for source in here.order[1:]:
            line_copy(k, 0, source).wait_recv()
            total = total + from_line[k, source].astype(jnp.float32)
        out_ref[tokens, :] = total.astype(jnp.bfloat16)

    def sums_sent(k):
        for i in range(4):
            core_copy(k, i).wait_send()
            for kind in range(3):
                plane_copy(k, i, kind, here.own, here.to_x).wait_send()
        for i in range(1, 4):
            line_copy(k, i, 0).wait_send()

    def send_core(k):
        for i in (3, 2, 1, 0):
            core_copy(k, i).start()

    moves = (
        lambda k, i: send_peers(k),
        along_line,
        beside,
        across,
        lambda k, i: all_rows(k),
        leave,
        pass_on,
        send_line,
        lambda k, i: finish(k),
        lambda k, i: send_core(k),
        lambda k, i: send_last(k),
        lambda k, i: pass_last(k),
    )

    def run(events):
        for event in events:
            moves[event // 100](event // 10 % 10, event % 10)

    tiles = units // 256
    steps = 2 * tiles + 2
    run(SCHEDULE[0])
    for copy in loads:
        copy.wait()

    @pl.loop(0, chunks)
    def _(k):
        for n in range(steps):
            if n < 2 * tiles:
                activate(k, core if n < tiles else 1 - core, n % tiles)
            elif n == 2 * tiles:
                for chunk in range(chunks):
                    pl.when(k == chunk)(functools.partial(rows_sent, chunk))
                lower(k, 1 - core)
            else:
                lower(k, core)
            for chunk in range(chunks):
                events = SCHEDULE[1 + chunk * steps + n]
                if events:
                    pl.when(k == chunk)(functools.partial(run, events))

    for k in range(chunks):
        sums_sent(k)
    for i in (1, 2, 3):
        for n in range(3):
            head_copy(n, i, here.z).wait_send()
        part_copy(0, i, None, here.z, False).wait_send()
        for g in (1, 2, 3):
            for k in range(chunks):
                part_copy(g, i, k, here.z, False).wait_send()


def local_block(
    queries,
    key_heads,
    value_heads,
    residual,
    lengths,
    routes,
    gate_weights,
    out_weight,
    norm_gain,
    w_gate,
    w_up,
    w_down,
):
    tokens, width = residual.shape[1:]
    line, size = lax.axis_size("seq"), ROWS
    chunks = tokens // size
    units = w_gate.shape[3]
    anywhere = pl.BlockSpec(memory_space=pl.ANY)
    inside = pl.BlockSpec(memory_space=pltpu.VMEM)
    scalars = pl.BlockSpec(memory_space=pltpu.SMEM)
    dma = pltpu.SemaphoreType.DMA
    half = jnp.bfloat16
    head_width, key_width = queries.shape[2] // line, key_heads.shape[2] // line
    whole = line * tokens
    result = pl.pallas_call(
        functools.partial(block_kernel, chunks, size),
        out_shape=jax.ShapeDtypeStruct((tokens, width), half),
        in_specs=[
            anywhere,
            anywhere,
            anywhere,
            inside,
            scalars,
            inside,
            inside,
            anywhere,
            inside,
            anywhere,
            anywhere,
            anywhere,
        ],
        out_specs=inside,
        scratch_shapes=[
            pltpu.VMEM((whole, head_width), half),
            pltpu.VMEM((whole, key_width), half),
            pltpu.VMEM((whole, key_width), half),
            pltpu.VMEM((whole, head_width), half),
            pltpu.VMEM((whole, width), half),
            pltpu.VMEM((line, tokens, width), half),
            pltpu.VMEM((tokens, width), half),
            pltpu.VMEM((tokens, width), jnp.float32),
            pltpu.VMEM((chunks, 32 * size, width + 128), half),
            pltpu.VMEM((chunks, 4, 4 * size, width), half),
            pltpu.VMEM((chunks, 12, size, width), half),
            pltpu.VMEM((chunks, 4, size, width), half),
            pltpu.VMEM(w_gate.shape[2:], half),
            pltpu.VMEM(w_up.shape[2:], half),
            pltpu.VMEM(w_down.shape[2:], half),
            pltpu.VMEM((32 * size, units), half),
            dma((10,)),
            dma((3, 3)),
            dma((3, line)),
            dma((28,)),
            dma((32,)),
            dma((3, 1 + 3 * chunks)),
            dma((line, 1 + 3 * chunks)),
            dma((1 + 3 * chunks,)),
            dma((chunks, 32)),
            dma((chunks, 32)),
            dma((chunks, 4)),
            dma((chunks, 4)),
            dma((chunks, 12)),
            dma((chunks, 12)),
            dma((chunks, 3)),
            dma((chunks, 4)),
        ],
        compiler_params=pltpu.CompilerParams(
            collective_id=0, has_side_effects=True, vmem_limit_bytes=67_000_000
        ),
    )(
        queries[0],
        key_heads[0],
        value_heads[0],
        residual[0],
        lengths,
        routes[0],
        gate_weights[0],
        out_weight,
        norm_gain[None, :],
        w_gate[0, 0],
        w_up[0, 0],
        w_down[0, 0],
    )
    return result[None]


def solution(mesh):
    plane = mesh.shape["exp"] == 8 and mesh.shape["seq"] == 4

    def local(*arguments):
        dense = plane and arguments[3].shape[1] == CHUNKS * ROWS
        return (local_block if dense else local_routed)(*arguments)

    return jax.shard_map(
        local,
        mesh=mesh,
        in_specs=(
            P("exp", "seq", None),
            P("exp", "seq", None),
            P("exp", "seq", None),
            P("exp", "seq", None),
            P("exp", None),
            P("exp", "seq", None),
            P("exp", "seq", None),
            P("seq", "exp"),
            P(),
            P("exp", "seq", None, None),
            P("exp", "seq", None, None),
            P("exp", "seq", None, None),
        ),
        out_specs=P("exp", "seq", None),
        check_vma=False,
    )
```

```python
import functools
import math

import jax
import jax.numpy as jnp
from jax import lax
from jax.experimental import pallas as pl
from jax.experimental.pallas import tpu as pltpu
from jax.sharding import PartitionSpec as P

HEAD_DIM = 128
EXP_COL = 2


epsilon = 1e-06


def episode_ids(length_row, position_count):
    bounds = jnp.cumsum(length_row)
    position = jnp.arange(position_count, dtype=jnp.int32)
    return jnp.sum((position[:, None] >= bounds[None, :]).astype(jnp.int32), axis=1)


def attend(query_rows, key_rows, value_rows, episode):
    row_count = query_rows.shape[0]
    groups = key_rows.shape[1] // HEAD_DIM
    per_group = query_rows.shape[1] // HEAD_DIM // groups
    q_heads = query_rows.reshape(row_count, groups, per_group, HEAD_DIM)
    k_heads = key_rows.reshape(row_count, groups, HEAD_DIM)
    v_heads = value_rows.reshape(row_count, groups, HEAD_DIM)
    scores = jnp.einsum(
        "tgpd,ugd->gptu", q_heads, k_heads, preferred_element_type=jnp.float32
    ) / math.sqrt(HEAD_DIM)
    position = jnp.arange(row_count, dtype=jnp.int32)
    allowed = (episode[:, None] == episode[None, :]) & (position[None, :] <= position[:, None])
    scores = jnp.where(allowed, scores, -jnp.inf)
    row_maximum = jnp.max(scores, axis=-1, keepdims=True)
    weights = jnp.exp(scores - row_maximum)
    probability = (weights / jnp.sum(weights, axis=-1, keepdims=True)).astype(jnp.bfloat16)
    mixed = jnp.einsum("gptu,ugd->tgpd", probability, v_heads, preferred_element_type=jnp.float32)
    return mixed.astype(jnp.bfloat16).reshape(row_count, groups * per_group * HEAD_DIM)


def local_routed(
    queries,
    key_heads,
    value_heads,
    residual,
    lengths,
    routes,
    gate_weights,
    out_weight,
    norm_gain,
    w_gate,
    w_up,
    w_down,
):
    seq_count = lax.axis_size("seq")
    columns = lax.axis_size("exp")
    token_count = residual.shape[1]
    model_width = residual.shape[2]
    whole_q, whole_k, whole_v = (
        lax.all_to_all(queries[0], "seq", split_axis=1, concat_axis=0, tiled=True),
        lax.all_to_all(key_heads[0], "seq", split_axis=1, concat_axis=0, tiled=True),
        lax.all_to_all(value_heads[0], "seq", split_axis=1, concat_axis=0, tiled=True),
    )
    episode = episode_ids(lengths[0], whole_q.shape[0])
    mixed = attend(whole_q, whole_k, whole_v, episode)
    head_partial = jnp.dot(
        mixed,
        lax.all_gather(out_weight, "exp", axis=1, tiled=True),
        preferred_element_type=jnp.float32,
    )
    projected = lax.psum_scatter(
        head_partial.astype(jnp.bfloat16), "seq", scatter_dimension=0, tiled=True
    ).astype(jnp.float32)
    hidden = residual[0].astype(jnp.float32) + projected
    inverse = lax.rsqrt(jnp.mean(hidden * hidden, axis=1, keepdims=True) + epsilon)
    normalized_rows = (hidden * inverse * norm_gain[None, :]).astype(jnp.bfloat16)
    routed = routes[0]
    node_count = routed.shape[1]
    capacity = max(2, 5 * token_count * node_count // (4 * columns))
    on_node = routed[:, :, None] == jnp.arange(columns, dtype=jnp.int32)[None, None, :]
    member = jnp.sum(on_node.astype(jnp.int32), axis=1)
    before = jnp.cumsum(member, axis=0) - member
    slot_lookup_index = (
        before[:, :, None] == jnp.arange(capacity, dtype=jnp.int32)[None, None, :]
    ) & (member[:, :, None] > 0)
    slot_flag_mask = slot_lookup_index.astype(jnp.bfloat16)
    outbound = jnp.einsum(
        "roj,rm->ojm", slot_flag_mask, normalized_rows, preferred_element_type=jnp.float32
    ).astype(jnp.bfloat16)
    gate_pair = gate_weights[0].reshape(token_count, node_count, EXP_COL).astype(jnp.float32)
    node_route_gate = jnp.einsum(
        "tnc,tne->tce", on_node.astype(jnp.float32), gate_pair, precision=lax.Precision.HIGHEST
    )
    slot_gate = jnp.einsum(
        "qnr,qny->nry",
        slot_lookup_index.astype(jnp.float32),
        node_route_gate,
        precision=lax.Precision.HIGHEST,
    ).astype(jnp.bfloat16)
    rows_in, gate_in = (
        lax.all_to_all(outbound, "exp", split_axis=0, concat_axis=0, tiled=True),
        lax.all_to_all(slot_gate, "exp", split_axis=0, concat_axis=0, tiled=True),
    )
    rows_all, gate_all = (
        lax.all_gather(rows_in, "seq", axis=0, tiled=True),
        lax.all_gather(gate_in, "seq", axis=0, tiled=True),
    )
    halves = seq_count // EXP_COL
    expert_pick = lax.axis_index("seq") // halves
    flat_rows = rows_all.reshape(-1, model_width)
    flat_gate = lax.dynamic_index_in_dim(
        gate_all.reshape(-1, EXP_COL), expert_pick, axis=1, keepdims=False
    )
    gate_block = w_gate[0, 0]
    up_block = w_up[0, 0]
    down_block = w_down[0, 0]
    gate_proj = jnp.dot(flat_rows, gate_block, preferred_element_type=jnp.float32)
    up_proj = jnp.dot(flat_rows, up_block, preferred_element_type=jnp.float32)
    activated = (jax.nn.silu(gate_proj) * up_proj).astype(jnp.bfloat16)
    partial_value = jnp.dot(activated, down_block, preferred_element_type=jnp.float32).astype(
        jnp.bfloat16
    )
    partial_value = lax.optimization_barrier(partial_value)
    node_sum = lax.psum_scatter(
        (partial_value.astype(jnp.float32) * flat_gate.astype(jnp.float32)[:, None]).astype(
            jnp.bfloat16
        ),
        "seq",
        scatter_dimension=0,
        tiled=True,
    )
    gathered_output = lax.all_to_all(
        node_sum.reshape(columns, capacity, model_width),
        "exp",
        split_axis=0,
        concat_axis=0,
        tiled=True,
    )
    mixture_expert_total = jnp.einsum(
        "gyr,yre->ge", slot_flag_mask, gathered_output, preferred_element_type=jnp.float32
    )
    return (hidden + mixture_expert_total).astype(jnp.bfloat16)[None]

ROWS = 16
CHUNKS = 4
MESH = pl.DeviceIdType.MESH


SPREAD = {1: 0, 2: 1, 3: 0}


SCHEDULE = (
    (
        1000, 1020, 1100, 0, 100, 102, 1010, 101, 200, 103, 1110, 201, 1120, 10, 110, 20, 202,
        300, 203, 112, 210, 302, 111, 303, 120, 301
    ),
    (),
    (),
    (113, 400),
    (310,),
    (211,),
    (122,),
    (1030, 900, 220, 121),
    (212, 222, 123, 502, 213, 503, 311, 500, 501, 312, 313),
    (1130,),
    (320,),
    (30, 410, 221),
    (130,),
    (601, 223),
    (322, 321),
    (603, 230, 132),
    (910, 602, 323),
    (701, 512, 131),
    (),
    (133, 420),
    (330, 511, 612),
    (),
    (),
    (513, 510, 920, 600, 332, 233),
    (333, 232, 231, 611, 610, 331, 702, 703),
    (613,),
    (521, 430, 520),
    (),
    (713, 523, 522, 712),
    (),
    (),
    (930, 622, 623),
    (
        621, 533, 711, 531, 722, 532, 633, 723, 632, 721, 810, 631, 530, 800, 733, 620, 732, 731,
        630, 820, 830
    ),
)


class Place:
    def __init__(self):
        self.z, self.e = lax.axis_index("seq"), lax.axis_index("exp")
        self.core = lax.rem(self.e, 2)
        x, y = lax.rem(lax.div(self.e, 2), 2), lax.div(self.e, 4)
        self.x, self.y = x, y
        half = lax.div(self.z, 2)
        self.turn = half
        self.mid = self.z + half * (3 - 2 * self.z)
        self.to_x = (self.z, self.e + 2 - 4 * x)
        self.to_y = (self.z, self.e + 4 - 8 * y)
        self.to_core = (self.z, self.e + 1 - 2 * self.core)
        self.order = [self.line(o) for o in (self.mid, 1 - self.mid, 2, 3)]
        self.peers = [(place, self.e) for place in self.order[1:]]
        self.own, self.by_x = y * 2 + x, y * 2 + 1 - x
        self.by_y, self.across = (1 - y) * 2 + x, (1 - y) * 2 + 1 - x

    def line(self, place):
        return place + self.turn * (3 - 2 * place)


def block_kernel(
    chunks,
    size,
    query_ref,
    key_ref,
    value_ref,
    residual_ref,
    length_ref,
    route_ref,
    weight_ref,
    project_ref,
    gain_ref,
    gate_hbm,
    up_hbm,
    down_hbm,
    out_ref,
    queries,
    keys,
    values,
    mixed,
    part,
    from_heads,
    from_near,
    hidden,
    held,
    from_core,
    from_plane,
    from_line,
    w_gate,
    w_up,
    w_down,
    activated,
    load_sem,
    head_send,
    head_recv,
    project_send,
    project_recv,
    part_send,
    part_recv,
    near_recv,
    row_send,
    row_recv,
    core_send,
    core_recv,
    plane_send,
    plane_recv,
    line_send,
    line_recv,
):
    here = Place()
    core = here.core
    width = hidden.shape[1]
    lane_count = lax.axis_size("exp") * EXP_COL
    tokens_here = chunks * size
    units = w_gate.shape[1]
    side = 16 * size

    barrier = pltpu.get_barrier_semaphore()
    for device in (here.to_x, here.to_y, here.to_core, *here.peers):
        pl.semaphore_signal(barrier, inc=1, device_id=device, device_id_type=MESH)

    loads = [
        pltpu.make_async_copy(source, target, load_sem.at[n])
        for n, (source, target) in enumerate(((down_hbm, w_down), (gate_hbm, w_gate), (up_hbm, w_up)))
    ]

    def remote(source, target, sent, got, device):
        return pltpu.make_async_remote_copy(
            src_ref=source,
            dst_ref=target,
            send_sem=sent,
            recv_sem=got,
            device_id=device,
            device_id_type=MESH,
        )

    def slot(which, i, quarter):
        return which * 16 + here.order[i] * 4 + quarter

    def columns_of(k):
        return pl.ds(0, held.shape[2] if k == 0 else width)

    heads = ((key_ref, keys), (value_ref, values), (query_ref, queries))

    def head_block(target, place):
        return target.at[pl.ds(pl.multiple_of(place * tokens_here, tokens_here), tokens_here)]

    def head_columns(source, target, place):
        span = target.shape[1]
        return source.at[:, pl.ds(pl.multiple_of(place * span, span), span)]

    def head_copy(n, i, source_place):
        source, target = heads[n]
        return remote(
            head_columns(source, target, here.order[i]),
            head_block(target, source_place),
            head_send.at[n, i - 1],
            head_recv.at[n, source_place],
            here.peers[i - 1],
        )

    head_loads = [
        pltpu.make_async_copy(
            head_columns(source, target, here.z), head_block(target, here.z), load_sem.at[3 + n]
        )
        for n, (source, target) in enumerate(heads)
    ]

    depth, span = project_ref.shape
    pieces = 4
    piece = depth // pieces

    def project_place(other, x, core, p):
        buffer = w_up if other else w_gate
        start = ((x * 2 + core) * pieces + p) * piece
        return buffer.at[pl.ds(pl.multiple_of(start, piece), piece), pl.ds(0, span)]

    def project_copy(source, other, x, core, p, n, device):
        return remote(
            source,
            project_place(other, x, core, p),
            project_send.at[n],
            project_recv.at[((other * 2 + x) * 2 + core) * pieces + p],
            device,
        )

    def own_piece(p):
        return project_ref.at[pl.ds(p * piece, piece)]

    own_projects = [
        pltpu.make_async_copy(
            own_piece(p), project_place(0, here.x, core, p), load_sem.at[6 + p]
        )
        for p in range(pieces)
    ]

    def got_piece(other, x, core, p):
        place = project_place(other, x, core, p)
        project_copy(place, other, x, core, p, 0, here.to_x).wait_recv()
        return place

    def project_x(p):
        place = got_piece(0, 1 - here.x, core, p)
        if p % 2 == 0:
            project_copy(place, 1, 1 - here.x, core, p, 12 + p // 2, here.to_y).start()
        project_copy(place, 0, 1 - here.x, core, p, 16 + p, here.to_core).start()

    def project_y(p):
        place = got_piece(1, here.x, core, p)
        if p % 2 == 1:
            project_copy(place, 1, here.x, core, p, 14 + p // 2, here.to_x).start()
        project_copy(place, 1, here.x, core, p, 20 + p, here.to_core).start()

    def project_across(p):
        place = got_piece(1, 1 - here.x, core, p)
        project_copy(place, 1, 1 - here.x, core, p, 24 + p, here.to_core).start()

    groups = (
        (0, here.x, here.own),
        (0, 1 - here.x, here.by_x),
        (1, here.x, here.by_y),
        (1, 1 - here.x, here.across),
    )

    def project(g):
        other, x, quarter = groups[g]
        for p in range(pieces):
            got_piece(other, x, 1 - core, p)
        buffer = w_up if other else w_gate

        @pl.loop(0, 4)
        def _(n):
            which, half = lax.div(n, 2), lax.rem(n, 2)
            rows = pl.ds(pl.multiple_of((x * 2 + which) * depth, depth), depth)
            weight = buffer[rows, pl.ds(pl.multiple_of(half * (span // 2), span // 2), span // 2)]
            total = jnp.dot(mixed[...], weight, preferred_element_type=jnp.float32)
            start = pl.multiple_of(quarter * 2 * span + n * (span // 2), span // 2)
            part[:, pl.ds(start, span // 2)] = total.astype(jnp.bfloat16)

    def part_copy(g, i, chunk, source_place, near):
        quarter = groups[g][2]
        columns = pl.ds(pl.multiple_of(quarter * 2 * span, 2 * span), 2 * span)
        count = tokens_here if chunk is None else size
        start = 0 if chunk is None else chunk * size
        n = 0 if chunk is None else 1 + (g - 1) * chunks + chunk
        rows = pl.ds(pl.multiple_of(here.order[i] * tokens_here + start, size), count)
        if near:
            target, got = from_near.at[pl.ds(start, count), columns], near_recv.at[n]
        else:
            target = from_heads.at[source_place, pl.ds(start, count), columns]
            got = part_recv.at[source_place, n]
        device = here.peers[0] if near else here.peers[i - 1]
        return remote(part.at[rows, columns], target, part_send.at[i - 1, n], got, device)

    def send_part(g, chunk=None):
        @pl.when(here.mid == 0)
        def _():
            part_copy(g, 3, chunk, here.z, True).start()

        for i in (2, 1):
            part_copy(g, i, chunk, here.z, False).start()

    def pass_part(g, chunk=None):
        quarter = groups[g][2]
        columns = pl.ds(pl.multiple_of(quarter * 2 * span, 2 * span), 2 * span)
        count = tokens_here if chunk is None else size
        start = 0 if chunk is None else chunk * size
        rows = pl.ds(pl.multiple_of(here.order[3] * tokens_here + start, size), count)

        @pl.when(here.mid == 1)
        def _():
            part_copy(g, 3, chunk, here.z, True).wait_recv()
            total = part[rows, columns].astype(jnp.float32)
            total = total + from_near[pl.ds(start, count), columns].astype(jnp.float32)
            part[rows, columns] = total.astype(jnp.bfloat16)
            part_copy(g, 3, chunk, here.z, False).start()

    def last_groups(k):
        return (1, 2, 3) if k + 1 == chunks else (3,)

    def send_last(k):
        for g in last_groups(k):
            send_part(g, k)

    def pass_last(k):
        for g in last_groups(k):
            pass_part(g, k)

    def attend():
        count = queries.shape[0]
        rows = lax.broadcasted_iota(jnp.int32, (count, count), 0)
        columns = lax.broadcasted_iota(jnp.int32, (count, count), 1)
        row_episode, column_episode = jnp.zeros_like(rows), jnp.zeros_like(rows)
        bound = 0
        for n in range(length_ref.shape[1]):
            bound = bound + length_ref[0, n]
            row_episode += (rows >= bound).astype(jnp.int32)
            column_episode += (columns >= bound).astype(jnp.int32)
        allowed = (row_episode == column_episode) & (columns <= rows)
        kept = jnp.where(allowed, 0.0, -jnp.inf)

        @pl.loop(0, queries.shape[1] // HEAD_DIM)
        def _(head):
            lanes = pl.ds(pl.multiple_of(head * HEAD_DIM, HEAD_DIM), HEAD_DIM)
            scores = lax.dot_general(
                queries[:, lanes],
                keys[...],
                (((1,), (1,)), ((), ())),
                preferred_element_type=jnp.float32,
            )
            scores = scores * (1.0 / math.sqrt(HEAD_DIM)) + kept
            weights = jnp.exp(scores - jnp.max(scores, axis=1, keepdims=True))
            share = (weights / jnp.sum(weights, axis=1, keepdims=True)).astype(jnp.bfloat16)
            value = jnp.dot(share, values[...], preferred_element_type=jnp.float32)
            mixed[:, lanes] = value.astype(jnp.bfloat16)

    def spread_gates():
        lanes = lax.broadcasted_iota(jnp.int32, (128, tokens_here), 0)
        tokens = lax.broadcasted_iota(jnp.int32, (128, tokens_here), 1)
        first = lax.div(tokens, size) * lane_count
        total = jnp.zeros(lanes.shape, jnp.float32)
        for n in range(route_ref.shape[0]):
            routed = route_ref[n : n + 1, :]
            for e in range(EXP_COL):
                gate = weight_ref[EXP_COL * n + e : EXP_COL * n + e + 1, :].astype(jnp.float32)
                total += jnp.where(lanes == first + routed * EXP_COL + e, gate, 0.0)
        row = lax.broadcasted_iota(jnp.int32, (size, tokens_here), 0)
        token = lax.broadcasted_iota(jnp.int32, (size, tokens_here), 1)
        pick = jnp.where(lax.rem(token, size) == row, 1.0, 0.0).astype(jnp.bfloat16)
        return lax.dot_general(
            pick,
            total.astype(jnp.bfloat16),
            (((1,), (1,)), ((), ())),
            preferred_element_type=jnp.float32,
        ).astype(jnp.bfloat16)

    def normalize(k):
        tokens = pl.ds(k * size, size)

        def got(place):
            if k == 0:
                part_copy(0, 1, None, place, False).wait_recv()
            for g in (1, 2, 3):
                part_copy(g, 1, k, place, False).wait_recv()
            return from_heads[place, tokens, :].astype(jnp.float32)

        mine = pl.ds(pl.multiple_of(here.z * tokens_here + k * size, size), size)
        total = residual_ref[tokens, :].astype(jnp.float32) + part[mine, :].astype(jnp.float32)
        hidden[tokens, :] = total + got(here.order[1]) + got(here.order[2])

        @pl.when(here.mid == 1)
        def _():
            hidden[tokens, :] = hidden[tokens, :] + got(here.order[3])

        total = hidden[tokens, :]
        inverse = lax.rsqrt(jnp.mean(total * total, axis=1, keepdims=True) + epsilon)
        rows = pl.ds(pl.multiple_of(slot(core, 0, here.own) * size, size), size)
        held[k, rows, pl.ds(0, width)] = (total * inverse * gain_ref[...]).astype(jnp.bfloat16)

    for copy in [loads[0], *head_loads, *own_projects]:
        copy.start()
    pl.semaphore_wait(barrier, 6)
    for n in range(3):
        for i in (1, 2, 3):
            head_copy(n, i, here.z).start()
    for p in range(pieces):
        project_copy(own_piece(p), 0, here.x, core, p, p, here.to_x).start()
        project_copy(own_piece(p), 1, here.x, core, p, 4 + p, here.to_y).start()
        project_copy(own_piece(p), 0, here.x, core, p, 8 + p, here.to_core).start()
    for p in range(2):
        project_x(p)
        project_y(p)
    for n in range(3):
        head_loads[n].wait()
        for i in (1, 2, 3):
            head_copy(n, i, here.order[i]).wait_recv()
    attend()
    for copy in own_projects:
        copy.wait()
    project(0)
    send_part(0)
    for p in range(2, pieces):
        project_x(p)
        project_y(p)
    project(1)
    project(2)
    for chunk in range(chunks - 1):
        send_part(1, chunk)
        send_part(2, chunk)
    own_rows = pl.ds(pl.multiple_of(slot(core, 0, here.own) * size, size), size)
    held[0, own_rows, pl.ds(width, 128)] = spread_gates()
    pass_part(0)
    for p in range(2):
        project_across(p)
    for chunk in range(chunks - 1):
        pass_part(1, chunk)
        pass_part(2, chunk)
    for p in range(2, pieces):
        project_across(p)
    project(3)
    for n in range(28):
        project_copy(own_piece(0), 0, here.x, core, 0, n, here.to_x).wait_send()
    for copy in loads[1:]:
        copy.start()

    def row_copy(k, which, n, device):
        block = held.at[k, pl.ds(pl.multiple_of(which * size, size), size), columns_of(k)]
        return pltpu.make_async_remote_copy(
            src_ref=block,
            dst_ref=block,
            send_sem=row_send.at[k, n],
            recv_sem=row_recv.at[k, which],
            device_id=device,
            device_id_type=MESH,
        )

    def send_peers(k):
        normalize(k)
        s = slot(core, 0, here.own)
        row_copy(k, s, 0, here.peers[0]).start()
        row_copy(k, s, 1, here.peers[1]).start()

        @pl.when(here.mid == 1)
        def _():
            row_copy(k, s, 2, here.peers[2]).start()

    def along_line(k, i):
        s = slot(core, i, here.own)
        if i > 0:
            row_copy(k, s, 0, here.peers[0]).wait_recv()
        if i == 3:

            @pl.when(here.mid == 1)
            def _():
                row_copy(k, s, 31, here.peers[0]).start()

        row_copy(k, s, 3 + i, here.to_x).start()
        row_copy(k, s, 9 + i, here.to_y).start()
        row_copy(k, s, 15 + i, here.to_core).start()

    def beside(k, i):
        s = slot(core, i, here.by_x)
        row_copy(k, s, 0, here.to_x).wait_recv()
        if i % 2 == 0 and k not in SPREAD or i == 0 and SPREAD.get(k) == 0:
            row_copy(k, s, 13 + i // 2, here.to_y).start()
        row_copy(k, s, 19 + i, here.to_core).start()
        s = slot(core, i, here.by_y)
        row_copy(k, s, 0, here.to_y).wait_recv()
        if i % 2 == 1 and k not in SPREAD or i == 0 and SPREAD.get(k) == 1:
            row_copy(k, s, 7 + i // 2, here.to_x).start()
        row_copy(k, s, 23 + i, here.to_core).start()

    def across(k, i):
        s = slot(core, i, here.across)
        row_copy(k, s, 0, here.to_x).wait_recv()
        if k in SPREAD and i == 0:
            row_copy(k, s, 32, here.peers[0]).start()
            row_copy(k, s, 33, here.peers[1]).start()
        if k in SPREAD and i in (0, 3):

            @pl.when(here.mid == 1)
            def _():
                row_copy(k, s, 34 + i // 3, here.peers[2 if i == 0 else 0]).start()

        row_copy(k, s, 27 + i, here.to_core).start()

    def all_rows(k):
        @pl.loop(0, 16)
        def _(n):
            row_copy(k, (1 - core) * 16 + n, 0, here.to_core).wait_recv()

    def rows_sent(k):
        always, middle = [0, 1, *range(3, 7), *range(9, 13), *range(15, 31)], [2, 31]
        if k in SPREAD:
            always += [32, 33, (13, 7)[SPREAD[k]]]
            middle += [34, 35]
        else:
            always += [7, 8, 13, 14]
        for n in always:
            row_copy(k, 0, n, here.to_core).wait_send()

        @pl.when(here.mid == 1)
        def _():
            for n in middle:
                row_copy(k, 0, n, here.to_core).wait_send()

    def activate(k, which, tile):
        rows = pl.ds(pl.multiple_of(which * side, side), side)
        columns = pl.ds(tile * 256, 256)
        tokens = held[k, rows, pl.ds(0, width)]
        gates = held[0, rows, pl.ds(width, 128)].astype(jnp.float32)
        lanes = lax.broadcasted_iota(jnp.int32, gates.shape, 1)
        lane = k * lane_count + here.e * EXP_COL + lax.div(here.z, 2)
        scale = jnp.sum(jnp.where(lanes == lane, gates, 0.0), axis=1, keepdims=True)
        gate = jnp.dot(tokens, w_gate[:, columns], preferred_element_type=jnp.float32)
        up = jnp.dot(tokens, w_up[:, columns], preferred_element_type=jnp.float32)
        value = gate / (1.0 + jnp.exp(-gate)) * up * scale
        activated[rows, columns] = value.astype(jnp.bfloat16)

    def lower(k, which):
        rows = pl.ds(pl.multiple_of(which * side, side), side)

        @pl.loop(0, width // 512)
        def _(tile):
            columns = pl.ds(pl.multiple_of(tile * 512, 512), 512)
            part = jnp.dot(activated[rows, :], w_down[:, columns], preferred_element_type=jnp.float32)
            held[k, rows, columns] = part.astype(jnp.bfloat16)

    def core_copy(k, i):
        def group(which):
            return pl.ds(pl.multiple_of((which * 16 + here.order[i] * 4) * size, 4 * size), 4 * size)

        return pltpu.make_async_remote_copy(
            src_ref=held.at[k, group(1 - core), pl.ds(0, width)],
            dst_ref=from_core.at[k, i],
            send_sem=core_send.at[k, i],
            recv_sem=core_recv.at[k, i],
            device_id=here.to_core,
            device_id_type=MESH,
        )

    def mine(k, i, quarter):
        return held.at[
            k, pl.ds(pl.multiple_of(slot(core, i, quarter) * size, size), size), pl.ds(0, width)
        ]

    def both(k, i, quarter):
        other = from_core[k, i, pl.ds(pl.multiple_of(quarter * size, size), size), :]
        return mine(k, i, quarter)[...].astype(jnp.float32) + other.astype(jnp.float32)

    def plane_copy(k, i, kind, quarter, device):
        return pltpu.make_async_remote_copy(
            src_ref=mine(k, i, quarter),
            dst_ref=from_plane.at[k, 4 * kind + i],
            send_sem=plane_send.at[k, 4 * kind + i],
            recv_sem=plane_recv.at[k, 4 * kind + i],
            device_id=device,
            device_id_type=MESH,
        )

    def links(i):
        if i % 2 == 0:
            return here.to_y, here.to_x, here.by_y, here.by_x
        return here.to_x, here.to_y, here.by_x, here.by_y

    def leave(k, i):
        first, _, direct, _ = links(i)
        core_copy(k, i).wait_recv()
        mine(k, i, here.across)[...] = both(k, i, here.across).astype(jnp.bfloat16)
        plane_copy(k, i, 0, here.across, first).start()
        mine(k, i, direct)[...] = both(k, i, direct).astype(jnp.bfloat16)
        plane_copy(k, i, 1, direct, first).start()

    def pass_on(k, i):
        first, second, _, onward = links(i)
        plane_copy(k, i, 0, onward, first).wait_recv()
        total = both(k, i, onward) + from_plane[k, i].astype(jnp.float32)
        mine(k, i, onward)[...] = total.astype(jnp.bfloat16)
        plane_copy(k, i, 2, onward, second).start()

    def line_copy(k, i, source):
        return pltpu.make_async_remote_copy(
            src_ref=mine(k, i, here.own),
            dst_ref=from_line.at[k, source],
            send_sem=line_send.at[k, max(i, 1) - 1],
            recv_sem=line_recv.at[k, source],
            device_id=here.peers[max(i, 1) - 1],
            device_id_type=MESH,
        )

    def line_sum(k, i):
        first, second, _, _ = links(i)
        plane_copy(k, i, 1, here.own, first).wait_recv()
        plane_copy(k, i, 2, here.own, second).wait_recv()
        total = both(k, i, here.own) + from_plane[k, 4 + i].astype(jnp.float32)
        return total + from_plane[k, 8 + i].astype(jnp.float32)

    def send_line(k, i):
        mine(k, i, here.own)[...] = line_sum(k, i).astype(jnp.bfloat16)
        line_copy(k, i, here.z).start()

    def finish(k):
        tokens = pl.ds(pl.multiple_of(k * size, size), size)
        total = hidden[tokens, :] + line_sum(k, 0)
        for source in here.order[1:]:
            line_copy(k, 0, source).wait_recv()
            total = total + from_line[k, source].astype(jnp.float32)
        out_ref[tokens, :] = total.astype(jnp.bfloat16)

    def sums_sent(k):
        for i in range(4):
            core_copy(k, i).wait_send()
            for kind in range(3):
                plane_copy(k, i, kind, here.own, here.to_x).wait_send()
        for i in range(1, 4):
            line_copy(k, i, 0).wait_send()

    def send_core(k):
        for i in (3, 2, 1, 0):
            core_copy(k, i).start()

    moves = (
        lambda k, i: send_peers(k),
        along_line,
        beside,
        across,
        lambda k, i: all_rows(k),
        leave,
        pass_on,
        send_line,
        lambda k, i: finish(k),
        lambda k, i: send_core(k),
        lambda k, i: send_last(k),
        lambda k, i: pass_last(k),
    )

    def run(events):
        for event in events:
            moves[event // 100](event // 10 % 10, event % 10)

    tiles = units // 256
    steps = 2 * tiles + 2
    run(SCHEDULE[0])
    for copy in loads:
        copy.wait()

    @pl.loop(0, chunks)
    def _(k):
        for n in range(steps):
            if n < 2 * tiles:
                activate(k, core if n < tiles else 1 - core, n % tiles)
            elif n == 2 * tiles:
                for chunk in range(chunks):
                    pl.when(k == chunk)(functools.partial(rows_sent, chunk))
                lower(k, 1 - core)
            else:
                lower(k, core)
            for chunk in range(chunks):
                events = SCHEDULE[1 + chunk * steps + n]
                if events:
                    pl.when(k == chunk)(functools.partial(run, events))

    for k in range(chunks):
        sums_sent(k)
    for i in (1, 2, 3):
        for n in range(3):
            head_copy(n, i, here.z).wait_send()
        part_copy(0, i, None, here.z, False).wait_send()
        for g in (1, 2, 3):
            for k in range(chunks):
                part_copy(g, i, k, here.z, False).wait_send()


def local_block(
    queries,
    key_heads,
    value_heads,
    residual,
    lengths,
    routes,
    gate_weights,
    out_weight,
    norm_gain,
    w_gate,
    w_up,
    w_down,
):
    tokens, width = residual.shape[1:]
    line, size = lax.axis_size("seq"), ROWS
    chunks = tokens // size
    units = w_gate.shape[3]
    anywhere = pl.BlockSpec(memory_space=pl.ANY)
    inside = pl.BlockSpec(memory_space=pltpu.VMEM)
    scalars = pl.BlockSpec(memory_space=pltpu.SMEM)
    dma = pltpu.SemaphoreType.DMA
    half = jnp.bfloat16
    head_width, key_width = queries.shape[2] // line, key_heads.shape[2] // line
    whole = line * tokens
    result = pl.pallas_call(
        functools.partial(block_kernel, chunks, size),
        out_shape=jax.ShapeDtypeStruct((tokens, width), half),
        in_specs=[
            anywhere,
            anywhere,
            anywhere,
            inside,
            scalars,
            inside,
            inside,
            anywhere,
            inside,
            anywhere,
            anywhere,
            anywhere,
        ],
        out_specs=inside,
        scratch_shapes=[
            pltpu.VMEM((whole, head_width), half),
            pltpu.VMEM((whole, key_width), half),
            pltpu.VMEM((whole, key_width), half),
            pltpu.VMEM((whole, head_width), half),
            pltpu.VMEM((whole, width), half),
            pltpu.VMEM((line, tokens, width), half),
            pltpu.VMEM((tokens, width), half),
            pltpu.VMEM((tokens, width), jnp.float32),
            pltpu.VMEM((chunks, 32 * size, width + 128), half),
            pltpu.VMEM((chunks, 4, 4 * size, width), half),
            pltpu.VMEM((chunks, 12, size, width), half),
            pltpu.VMEM((chunks, 4, size, width), half),
            pltpu.VMEM(w_gate.shape[2:], half),
            pltpu.VMEM(w_up.shape[2:], half),
            pltpu.VMEM(w_down.shape[2:], half),
            pltpu.VMEM((32 * size, units), half),
            dma((10,)),
            dma((3, 3)),
            dma((3, line)),
            dma((28,)),
            dma((32,)),
            dma((3, 1 + 3 * chunks)),
            dma((line, 1 + 3 * chunks)),
            dma((1 + 3 * chunks,)),
            dma((chunks, 36)),
            dma((chunks, 32)),
            dma((chunks, 4)),
            dma((chunks, 4)),
            dma((chunks, 12)),
            dma((chunks, 12)),
            dma((chunks, 3)),
            dma((chunks, 4)),
        ],
        compiler_params=pltpu.CompilerParams(
            collective_id=0, has_side_effects=True, vmem_limit_bytes=67_000_000
        ),
    )(
        queries[0],
        key_heads[0],
        value_heads[0],
        residual[0],
        lengths,
        routes[0].T,
        gate_weights[0].T,
        out_weight,
        norm_gain[None, :],
        w_gate[0, 0],
        w_up[0, 0],
        w_down[0, 0],
    )
    return result[None]


def solution(mesh):
    plane = mesh.shape["exp"] == 8 and mesh.shape["seq"] == 4

    def local(*arguments):
        dense = plane and arguments[3].shape[1] == CHUNKS * ROWS
        return (local_block if dense else local_routed)(*arguments)

    return jax.shard_map(
        local,
        mesh=mesh,
        in_specs=(
            P("exp", "seq", None),
            P("exp", "seq", None),
            P("exp", "seq", None),
            P("exp", "seq", None),
            P("exp", None),
            P("exp", "seq", None),
            P("exp", "seq", None),
            P("seq", "exp"),
            P(),
            P("exp", "seq", None, None),
            P("exp", "seq", None, None),
            P("exp", "seq", None, None),
        ),
        out_specs=P("exp", "seq", None),
        check_vma=False,
    )
```

```python
import functools
import math

import jax
import jax.numpy as jnp
from jax import lax
from jax.experimental import pallas as pl
from jax.experimental.pallas import tpu as pltpu
from jax.sharding import PartitionSpec as P

HEAD_DIM = 128
EXP_COL = 2


epsilon = 1e-06


def episode_ids(length_row, position_count):
    bounds = jnp.cumsum(length_row)
    position = jnp.arange(position_count, dtype=jnp.int32)
    return jnp.sum((position[:, None] >= bounds[None, :]).astype(jnp.int32), axis=1)


def attend(query_rows, key_rows, value_rows, episode):
    row_count = query_rows.shape[0]
    groups = key_rows.shape[1] // HEAD_DIM
    per_group = query_rows.shape[1] // HEAD_DIM // groups
    q_heads = query_rows.reshape(row_count, groups, per_group, HEAD_DIM)
    k_heads = key_rows.reshape(row_count, groups, HEAD_DIM)
    v_heads = value_rows.reshape(row_count, groups, HEAD_DIM)
    scores = jnp.einsum(
        "tgpd,ugd->gptu", q_heads, k_heads, preferred_element_type=jnp.float32
    ) / math.sqrt(HEAD_DIM)
    position = jnp.arange(row_count, dtype=jnp.int32)
    allowed = (episode[:, None] == episode[None, :]) & (position[None, :] <= position[:, None])
    scores = jnp.where(allowed, scores, -jnp.inf)
    row_maximum = jnp.max(scores, axis=-1, keepdims=True)
    weights = jnp.exp(scores - row_maximum)
    probability = (weights / jnp.sum(weights, axis=-1, keepdims=True)).astype(jnp.bfloat16)
    mixed = jnp.einsum("gptu,ugd->tgpd", probability, v_heads, preferred_element_type=jnp.float32)
    return mixed.astype(jnp.bfloat16).reshape(row_count, groups * per_group * HEAD_DIM)


def local_routed(
    queries,
    key_heads,
    value_heads,
    residual,
    lengths,
    routes,
    gate_weights,
    out_weight,
    norm_gain,
    w_gate,
    w_up,
    w_down,
):
    seq_count = lax.axis_size("seq")
    columns = lax.axis_size("exp")
    token_count = residual.shape[1]
    model_width = residual.shape[2]
    whole_q, whole_k, whole_v = (
        lax.all_to_all(queries[0], "seq", split_axis=1, concat_axis=0, tiled=True),
        lax.all_to_all(key_heads[0], "seq", split_axis=1, concat_axis=0, tiled=True),
        lax.all_to_all(value_heads[0], "seq", split_axis=1, concat_axis=0, tiled=True),
    )
    episode = episode_ids(lengths[0], whole_q.shape[0])
    mixed = attend(whole_q, whole_k, whole_v, episode)
    head_partial = jnp.dot(
        mixed,
        lax.all_gather(out_weight, "exp", axis=1, tiled=True),
        preferred_element_type=jnp.float32,
    )
    projected = lax.psum_scatter(
        head_partial.astype(jnp.bfloat16), "seq", scatter_dimension=0, tiled=True
    ).astype(jnp.float32)
    hidden = residual[0].astype(jnp.float32) + projected
    inverse = lax.rsqrt(jnp.mean(hidden * hidden, axis=1, keepdims=True) + epsilon)
    normalized_rows = (hidden * inverse * norm_gain[None, :]).astype(jnp.bfloat16)
    routed = routes[0]
    node_count = routed.shape[1]
    capacity = max(2, 5 * token_count * node_count // (4 * columns))
    on_node = routed[:, :, None] == jnp.arange(columns, dtype=jnp.int32)[None, None, :]
    member = jnp.sum(on_node.astype(jnp.int32), axis=1)
    before = jnp.cumsum(member, axis=0) - member
    slot_lookup_index = (
        before[:, :, None] == jnp.arange(capacity, dtype=jnp.int32)[None, None, :]
    ) & (member[:, :, None] > 0)
    slot_flag_mask = slot_lookup_index.astype(jnp.bfloat16)
    outbound = jnp.einsum(
        "roj,rm->ojm", slot_flag_mask, normalized_rows, preferred_element_type=jnp.float32
    ).astype(jnp.bfloat16)
    gate_pair = gate_weights[0].reshape(token_count, node_count, EXP_COL).astype(jnp.float32)
    node_route_gate = jnp.einsum(
        "tnc,tne->tce", on_node.astype(jnp.float32), gate_pair, precision=lax.Precision.HIGHEST
    )
    slot_gate = jnp.einsum(
        "qnr,qny->nry",
        slot_lookup_index.astype(jnp.float32),
        node_route_gate,
        precision=lax.Precision.HIGHEST,
    ).astype(jnp.bfloat16)
    rows_in, gate_in = (
        lax.all_to_all(outbound, "exp", split_axis=0, concat_axis=0, tiled=True),
        lax.all_to_all(slot_gate, "exp", split_axis=0, concat_axis=0, tiled=True),
    )
    rows_all, gate_all = (
        lax.all_gather(rows_in, "seq", axis=0, tiled=True),
        lax.all_gather(gate_in, "seq", axis=0, tiled=True),
    )
    halves = seq_count // EXP_COL
    expert_pick = lax.axis_index("seq") // halves
    flat_rows = rows_all.reshape(-1, model_width)
    flat_gate = lax.dynamic_index_in_dim(
        gate_all.reshape(-1, EXP_COL), expert_pick, axis=1, keepdims=False
    )
    gate_block = w_gate[0, 0]
    up_block = w_up[0, 0]
    down_block = w_down[0, 0]
    gate_proj = jnp.dot(flat_rows, gate_block, preferred_element_type=jnp.float32)
    up_proj = jnp.dot(flat_rows, up_block, preferred_element_type=jnp.float32)
    activated = (jax.nn.silu(gate_proj) * up_proj).astype(jnp.bfloat16)
    partial_value = jnp.dot(activated, down_block, preferred_element_type=jnp.float32).astype(
        jnp.bfloat16
    )
    partial_value = lax.optimization_barrier(partial_value)
    node_sum = lax.psum_scatter(
        (partial_value.astype(jnp.float32) * flat_gate.astype(jnp.float32)[:, None]).astype(
            jnp.bfloat16
        ),
        "seq",
        scatter_dimension=0,
        tiled=True,
    )
    gathered_output = lax.all_to_all(
        node_sum.reshape(columns, capacity, model_width),
        "exp",
        split_axis=0,
        concat_axis=0,
        tiled=True,
    )
    mixture_expert_total = jnp.einsum(
        "gyr,yre->ge", slot_flag_mask, gathered_output, preferred_element_type=jnp.float32
    )
    return (hidden + mixture_expert_total).astype(jnp.bfloat16)[None]

ROWS = 16
CHUNKS = 4
MESH = pl.DeviceIdType.MESH


GATHER = {2: 0}


SPREAD = {1: 0, 2: 1, 3: 0}


SCHEDULE = (
    (
        1000, 1100, 1020, 0, 1010, 100, 102, 101, 200, 1120, 1110, 103, 10, 20, 202, 201, 300,
        203, 110, 301, 302, 120, 303
    ),
    (),
    (210, 122, 1030),
    (400, 121, 113, 112, 111, 220, 310),
    (),
    (),
    (),
    (900,),
    (123, 311, 503, 222, 212, 1130, 502, 221, 500, 213, 211, 312, 501, 313),
    (320, 30, 130),
    (410,),
    (),
    (),
    (223,),
    (),
    (603,),
    (602, 230, 321, 322, 323),
    (132, 420, 910, 133),
    (330,),
    (131, 703, 513, 232),
    (511, 512, 510),
    (231,),
    (233,),
    (702, 333, 920, 613, 601, 332, 331),
    (610, 523),
    (522,),
    (521, 430, 621),
    (713, 612),
    (520, 701),
    (622, 600),
    (623,),
    (611, 712, 930, 1220),
    (
        533, 722, 531, 532, 711, 723, 721, 633, 631, 800, 632, 620, 733, 530, 810, 731, 732, 630,
        820, 830
    ),
)


class Place:
    def __init__(self):
        self.z, self.e = lax.axis_index("seq"), lax.axis_index("exp")
        self.core = lax.rem(self.e, 2)
        x, y = lax.rem(lax.div(self.e, 2), 2), lax.div(self.e, 4)
        self.x, self.y = x, y
        half = lax.div(self.z, 2)
        self.turn = half
        self.mid = self.z + half * (3 - 2 * self.z)
        self.to_x = (self.z, self.e + 2 - 4 * x)
        self.to_y = (self.z, self.e + 4 - 8 * y)
        self.to_core = (self.z, self.e + 1 - 2 * self.core)
        self.order = [self.line(o) for o in (self.mid, 1 - self.mid, 2, 3)]
        self.peers = [(place, self.e) for place in self.order[1:]]
        self.own, self.by_x = y * 2 + x, y * 2 + 1 - x
        self.by_y, self.across = (1 - y) * 2 + x, (1 - y) * 2 + 1 - x

    def line(self, place):
        return place + self.turn * (3 - 2 * place)


def block_kernel(
    chunks,
    size,
    query_ref,
    key_ref,
    value_ref,
    residual_ref,
    length_ref,
    route_ref,
    weight_ref,
    project_ref,
    gain_ref,
    gate_hbm,
    up_hbm,
    down_hbm,
    out_ref,
    queries,
    keys,
    values,
    mixed,
    part,
    from_heads,
    from_near,
    hidden,
    held,
    from_core,
    from_plane,
    from_line,
    w_gate,
    w_up,
    w_down,
    activated,
    load_sem,
    head_send,
    head_recv,
    project_send,
    project_recv,
    part_send,
    part_recv,
    near_recv,
    row_send,
    row_recv,
    core_send,
    core_recv,
    plane_send,
    plane_recv,
    line_send,
    line_recv,
):
    here = Place()
    core = here.core
    width = hidden.shape[1]
    lane_count = lax.axis_size("exp") * EXP_COL
    tokens_here = chunks * size
    units = w_gate.shape[1]
    side = 16 * size

    barrier = pltpu.get_barrier_semaphore()
    for device in (here.to_x, here.to_y, here.to_core, *here.peers):
        pl.semaphore_signal(barrier, inc=1, device_id=device, device_id_type=MESH)

    loads = [
        pltpu.make_async_copy(source, target, load_sem.at[n])
        for n, (source, target) in enumerate(((down_hbm, w_down), (gate_hbm, w_gate), (up_hbm, w_up)))
    ]

    def remote(source, target, sent, got, device):
        return pltpu.make_async_remote_copy(
            src_ref=source,
            dst_ref=target,
            send_sem=sent,
            recv_sem=got,
            device_id=device,
            device_id_type=MESH,
        )

    def slot(which, i, quarter):
        return which * 16 + here.order[i] * 4 + quarter

    def columns_of(k):
        return pl.ds(0, held.shape[2] if k == 0 else width)

    heads = ((key_ref, keys), (value_ref, values), (query_ref, queries))

    def head_block(target, place):
        return target.at[pl.ds(pl.multiple_of(place * tokens_here, tokens_here), tokens_here)]

    def head_columns(source, target, place):
        span = target.shape[1]
        return source.at[:, pl.ds(pl.multiple_of(place * span, span), span)]

    def head_copy(n, i, source_place):
        source, target = heads[n]
        return remote(
            head_columns(source, target, here.order[i]),
            head_block(target, source_place),
            head_send.at[n, i - 1],
            head_recv.at[n, source_place],
            here.peers[i - 1],
        )

    head_loads = [
        pltpu.make_async_copy(
            head_columns(source, target, here.z), head_block(target, here.z), load_sem.at[3 + n]
        )
        for n, (source, target) in enumerate(heads)
    ]

    depth, span = project_ref.shape
    pieces = 4
    piece = depth // pieces

    def project_place(other, x, core, p):
        buffer = w_up if other else w_gate
        start = ((x * 2 + core) * pieces + p) * piece
        return buffer.at[pl.ds(pl.multiple_of(start, piece), piece), pl.ds(0, span)]

    def project_copy(source, other, x, core, p, n, device):
        return remote(
            source,
            project_place(other, x, core, p),
            project_send.at[n],
            project_recv.at[((other * 2 + x) * 2 + core) * pieces + p],
            device,
        )

    def own_piece(p):
        return project_ref.at[pl.ds(p * piece, piece)]

    own_projects = [
        pltpu.make_async_copy(
            own_piece(p), project_place(0, here.x, core, p), load_sem.at[6 + p]
        )
        for p in range(pieces)
    ]

    def got_piece(other, x, core, p):
        place = project_place(other, x, core, p)
        project_copy(place, other, x, core, p, 0, here.to_x).wait_recv()
        return place

    def project_x(p):
        place = got_piece(0, 1 - here.x, core, p)
        if p % 2 == 0:
            project_copy(place, 1, 1 - here.x, core, p, 12 + p // 2, here.to_y).start()
        project_copy(place, 0, 1 - here.x, core, p, 16 + p, here.to_core).start()

    def project_y(p):
        place = got_piece(1, here.x, core, p)
        if p % 2 == 1:
            project_copy(place, 1, here.x, core, p, 14 + p // 2, here.to_x).start()
        project_copy(place, 1, here.x, core, p, 20 + p, here.to_core).start()

    def project_across(p):
        place = got_piece(1, 1 - here.x, core, p)
        project_copy(place, 1, 1 - here.x, core, p, 24 + p, here.to_core).start()

    groups = (
        (0, here.x, here.own),
        (0, 1 - here.x, here.by_x),
        (1, here.x, here.by_y),
        (1, 1 - here.x, here.across),
    )

    def project(g):
        other, x, quarter = groups[g]
        for p in range(pieces):
            got_piece(other, x, 1 - core, p)
        buffer = w_up if other else w_gate

        @pl.loop(0, 4)
        def _(n):
            which, half = lax.div(n, 2), lax.rem(n, 2)
            rows = pl.ds(pl.multiple_of((x * 2 + which) * depth, depth), depth)
            weight = buffer[rows, pl.ds(pl.multiple_of(half * (span // 2), span // 2), span // 2)]
            total = jnp.dot(mixed[...], weight, preferred_element_type=jnp.float32)
            start = pl.multiple_of(quarter * 2 * span + n * (span // 2), span // 2)
            part[:, pl.ds(start, span // 2)] = total.astype(jnp.bfloat16)

    def part_copy(g, i, chunk, source_place, near):
        quarter = groups[g][2]
        columns = pl.ds(pl.multiple_of(quarter * 2 * span, 2 * span), 2 * span)
        count = tokens_here if chunk is None else size
        start = 0 if chunk is None else chunk * size
        n = 0 if chunk is None else 1 + (g - 1) * chunks + chunk
        rows = pl.ds(pl.multiple_of(here.order[i] * tokens_here + start, size), count)
        if near:
            target, got = from_near.at[pl.ds(start, count), columns], near_recv.at[n]
        else:
            target = from_heads.at[source_place, pl.ds(start, count), columns]
            got = part_recv.at[source_place, n]
        device = here.peers[0] if near else here.peers[i - 1]
        return remote(part.at[rows, columns], target, part_send.at[i - 1, n], got, device)

    def send_part(g, chunk=None):
        @pl.when(here.mid == 0)
        def _():
            part_copy(g, 3, chunk, here.z, True).start()

        for i in (2, 1):
            part_copy(g, i, chunk, here.z, False).start()

    def pass_part(g, chunk=None):
        quarter = groups[g][2]
        columns = pl.ds(pl.multiple_of(quarter * 2 * span, 2 * span), 2 * span)
        count = tokens_here if chunk is None else size
        start = 0 if chunk is None else chunk * size
        rows = pl.ds(pl.multiple_of(here.order[3] * tokens_here + start, size), count)

        @pl.when(here.mid == 1)
        def _():
            part_copy(g, 3, chunk, here.z, True).wait_recv()
            total = part[rows, columns].astype(jnp.float32)
            total = total + from_near[pl.ds(start, count), columns].astype(jnp.float32)
            part[rows, columns] = total.astype(jnp.bfloat16)
            part_copy(g, 3, chunk, here.z, False).start()

    def last_groups(k):
        return (1, 2, 3) if k + 1 == chunks else (3,)

    def send_last(k):
        for g in last_groups(k):
            send_part(g, k)

    def pass_last(k):
        for g in last_groups(k):
            pass_part(g, k)

    def attend():
        count = queries.shape[0]
        rows = lax.broadcasted_iota(jnp.int32, (count, count), 0)
        columns = lax.broadcasted_iota(jnp.int32, (count, count), 1)
        row_episode, column_episode = jnp.zeros_like(rows), jnp.zeros_like(rows)
        bound = 0
        for n in range(length_ref.shape[1]):
            bound = bound + length_ref[0, n]
            row_episode += (rows >= bound).astype(jnp.int32)
            column_episode += (columns >= bound).astype(jnp.int32)
        allowed = (row_episode == column_episode) & (columns <= rows)
        kept = jnp.where(allowed, 0.0, -jnp.inf)

        @pl.loop(0, queries.shape[1] // HEAD_DIM)
        def _(head):
            lanes = pl.ds(pl.multiple_of(head * HEAD_DIM, HEAD_DIM), HEAD_DIM)
            scores = lax.dot_general(
                queries[:, lanes],
                keys[...],
                (((1,), (1,)), ((), ())),
                preferred_element_type=jnp.float32,
            )
            scores = scores * (1.0 / math.sqrt(HEAD_DIM)) + kept
            weights = jnp.exp(scores - jnp.max(scores, axis=1, keepdims=True))
            share = (weights / jnp.sum(weights, axis=1, keepdims=True)).astype(jnp.bfloat16)
            value = jnp.dot(share, values[...], preferred_element_type=jnp.float32)
            mixed[:, lanes] = value.astype(jnp.bfloat16)

    def spread_gates():
        lanes = lax.broadcasted_iota(jnp.int32, (128, tokens_here), 0)
        tokens = lax.broadcasted_iota(jnp.int32, (128, tokens_here), 1)
        first = lax.div(tokens, size) * lane_count
        total = jnp.zeros(lanes.shape, jnp.float32)
        for n in range(route_ref.shape[0]):
            routed = route_ref[n : n + 1, :]
            for e in range(EXP_COL):
                gate = weight_ref[EXP_COL * n + e : EXP_COL * n + e + 1, :].astype(jnp.float32)
                total += jnp.where(lanes == first + routed * EXP_COL + e, gate, 0.0)
        row = lax.broadcasted_iota(jnp.int32, (size, tokens_here), 0)
        token = lax.broadcasted_iota(jnp.int32, (size, tokens_here), 1)
        pick = jnp.where(lax.rem(token, size) == row, 1.0, 0.0).astype(jnp.bfloat16)
        return lax.dot_general(
            pick,
            total.astype(jnp.bfloat16),
            (((1,), (1,)), ((), ())),
            preferred_element_type=jnp.float32,
        ).astype(jnp.bfloat16)

    def normalize(k):
        tokens = pl.ds(k * size, size)

        def got(place):
            if k == 0:
                part_copy(0, 1, None, place, False).wait_recv()
            for g in (1, 2, 3):
                part_copy(g, 1, k, place, False).wait_recv()
            return from_heads[place, tokens, :].astype(jnp.float32)

        mine = pl.ds(pl.multiple_of(here.z * tokens_here + k * size, size), size)
        total = residual_ref[tokens, :].astype(jnp.float32) + part[mine, :].astype(jnp.float32)
        hidden[tokens, :] = total + got(here.order[1]) + got(here.order[2])

        @pl.when(here.mid == 1)
        def _():
            hidden[tokens, :] = hidden[tokens, :] + got(here.order[3])

        total = hidden[tokens, :]
        inverse = lax.rsqrt(jnp.mean(total * total, axis=1, keepdims=True) + epsilon)
        rows = pl.ds(pl.multiple_of(slot(core, 0, here.own) * size, size), size)
        held[k, rows, pl.ds(0, width)] = (total * inverse * gain_ref[...]).astype(jnp.bfloat16)

    for copy in [loads[0], *head_loads, *own_projects]:
        copy.start()
    pl.semaphore_wait(barrier, 6)
    for n in range(3):
        for i in (1, 2, 3):
            head_copy(n, i, here.z).start()
    for p in range(pieces):
        project_copy(own_piece(p), 0, here.x, core, p, p, here.to_x).start()
        project_copy(own_piece(p), 1, here.x, core, p, 4 + p, here.to_y).start()
        project_copy(own_piece(p), 0, here.x, core, p, 8 + p, here.to_core).start()
    for p in range(2):
        project_x(p)
        project_y(p)
    for n in range(3):
        head_loads[n].wait()
        for i in (1, 2, 3):
            head_copy(n, i, here.order[i]).wait_recv()
    attend()
    for copy in own_projects:
        copy.wait()
    project(0)
    send_part(0)
    for p in range(2, pieces):
        project_x(p)
        project_y(p)
    project(1)
    project(2)
    for chunk in range(chunks - 1):
        send_part(1, chunk)
        send_part(2, chunk)
    own_rows = pl.ds(pl.multiple_of(slot(core, 0, here.own) * size, size), size)
    held[0, own_rows, pl.ds(width, 128)] = spread_gates()
    pass_part(0)
    for p in range(2):
        project_across(p)
    for chunk in range(chunks - 1):
        pass_part(1, chunk)
        pass_part(2, chunk)
    for p in range(2, pieces):
        project_across(p)
    project(3)
    for n in range(28):
        project_copy(own_piece(0), 0, here.x, core, 0, n, here.to_x).wait_send()
    for copy in loads[1:]:
        copy.start()

    def row_copy(k, which, n, device):
        block = held.at[k, pl.ds(pl.multiple_of(which * size, size), size), columns_of(k)]
        return pltpu.make_async_remote_copy(
            src_ref=block,
            dst_ref=block,
            send_sem=row_send.at[k, n],
            recv_sem=row_recv.at[k, which],
            device_id=device,
            device_id_type=MESH,
        )

    def send_peers(k):
        normalize(k)
        s = slot(core, 0, here.own)
        row_copy(k, s, 0, here.peers[0]).start()
        row_copy(k, s, 1, here.peers[1]).start()

        @pl.when(here.mid == 1)
        def _():
            row_copy(k, s, 2, here.peers[2]).start()

    def along_line(k, i):
        s = slot(core, i, here.own)
        if i > 0:
            row_copy(k, s, 0, here.peers[0]).wait_recv()
        if i == 3:

            @pl.when(here.mid == 1)
            def _():
                row_copy(k, s, 31, here.peers[0]).start()

        row_copy(k, s, 3 + i, here.to_x).start()
        row_copy(k, s, 9 + i, here.to_y).start()
        row_copy(k, s, 15 + i, here.to_core).start()

    def beside(k, i):
        s = slot(core, i, here.by_x)
        row_copy(k, s, 0, here.to_x).wait_recv()
        if i % 2 == 0 and k not in SPREAD or i == 0 and SPREAD.get(k) == 0:
            row_copy(k, s, 13 + i // 2, here.to_y).start()
        row_copy(k, s, 19 + i, here.to_core).start()
        s = slot(core, i, here.by_y)
        row_copy(k, s, 0, here.to_y).wait_recv()
        if i % 2 == 1 and k not in SPREAD or i == 0 and SPREAD.get(k) == 1:
            row_copy(k, s, 7 + i // 2, here.to_x).start()
        row_copy(k, s, 23 + i, here.to_core).start()

    def across(k, i):
        s = slot(core, i, here.across)
        row_copy(k, s, 0, here.to_x).wait_recv()
        if k in SPREAD and i == 0:
            row_copy(k, s, 32, here.peers[0]).start()
            row_copy(k, s, 33, here.peers[1]).start()
        if k in SPREAD and i in (0, 3):

            @pl.when(here.mid == 1)
            def _():
                row_copy(k, s, 34 + i // 3, here.peers[2 if i == 0 else 0]).start()

        row_copy(k, s, 27 + i, here.to_core).start()

    def all_rows(k):
        @pl.loop(0, 16)
        def _(n):
            row_copy(k, (1 - core) * 16 + n, 0, here.to_core).wait_recv()

    def rows_sent(k):
        always, middle = [0, 1, *range(3, 7), *range(9, 13), *range(15, 31)], [2, 31]
        if k in SPREAD:
            always += [32, 33, (13, 7)[SPREAD[k]]]
            middle += [34, 35]
        else:
            always += [7, 8, 13, 14]
        for n in always:
            row_copy(k, 0, n, here.to_core).wait_send()

        @pl.when(here.mid == 1)
        def _():
            for n in middle:
                row_copy(k, 0, n, here.to_core).wait_send()

    def activate(k, which, tile):
        rows = pl.ds(pl.multiple_of(which * side, side), side)
        columns = pl.ds(tile * 256, 256)
        tokens = held[k, rows, pl.ds(0, width)]
        gates = held[0, rows, pl.ds(width, 128)].astype(jnp.float32)
        lanes = lax.broadcasted_iota(jnp.int32, gates.shape, 1)
        lane = k * lane_count + here.e * EXP_COL + lax.div(here.z, 2)
        scale = jnp.sum(jnp.where(lanes == lane, gates, 0.0), axis=1, keepdims=True)
        gate = jnp.dot(tokens, w_gate[:, columns], preferred_element_type=jnp.float32)
        up = jnp.dot(tokens, w_up[:, columns], preferred_element_type=jnp.float32)
        value = gate / (1.0 + jnp.exp(-gate)) * up * scale
        activated[rows, columns] = value.astype(jnp.bfloat16)

    def lower(k, which):
        rows = pl.ds(pl.multiple_of(which * side, side), side)

        @pl.loop(0, width // 512)
        def _(tile):
            columns = pl.ds(pl.multiple_of(tile * 512, 512), 512)
            part = jnp.dot(activated[rows, :], w_down[:, columns], preferred_element_type=jnp.float32)
            held[k, rows, columns] = part.astype(jnp.bfloat16)

    def core_copy(k, i):
        def group(which):
            return pl.ds(pl.multiple_of((which * 16 + here.order[i] * 4) * size, 4 * size), 4 * size)

        return pltpu.make_async_remote_copy(
            src_ref=held.at[k, group(1 - core), pl.ds(0, width)],
            dst_ref=from_core.at[k, i],
            send_sem=core_send.at[k, i],
            recv_sem=core_recv.at[k, i],
            device_id=here.to_core,
            device_id_type=MESH,
        )

    def mine(k, i, quarter):
        return held.at[
            k, pl.ds(pl.multiple_of(slot(core, i, quarter) * size, size), size), pl.ds(0, width)
        ]

    def both(k, i, quarter):
        other = from_core[k, i, pl.ds(pl.multiple_of(quarter * size, size), size), :]
        return mine(k, i, quarter)[...].astype(jnp.float32) + other.astype(jnp.float32)

    def plane_copy(k, i, kind, quarter, device):
        return pltpu.make_async_remote_copy(
            src_ref=mine(k, i, quarter),
            dst_ref=from_plane.at[k, 4 * kind + i],
            send_sem=plane_send.at[k, 4 * kind + i],
            recv_sem=plane_recv.at[k, 4 * kind + i],
            device_id=device,
            device_id_type=MESH,
        )

    def links(k, i):
        if (i % 2 if i or k not in GATHER else GATHER[k]) == 0:
            return here.to_y, here.to_x, here.by_y, here.by_x
        return here.to_x, here.to_y, here.by_x, here.by_y

    def cross_copy(k, i, source, target):
        place = 1 + lax.rem(source - target + 3, 4)
        return remote(
            mine(k, i, here.across),
            from_plane.at[k, place],
            plane_send.at[k, i],
            plane_recv.at[k, place],
            here.peers[i - 1],
        )

    def leave(k, i):
        first, _, direct, _ = links(k, i)
        core_copy(k, i).wait_recv()
        if k not in GATHER or i > 0:
            mine(k, i, here.across)[...] = both(k, i, here.across).astype(jnp.bfloat16)
            if k in GATHER:
                cross_copy(k, i, here.z, here.order[i]).start()
            else:
                plane_copy(k, i, 0, here.across, first).start()
        mine(k, i, direct)[...] = both(k, i, direct).astype(jnp.bfloat16)
        plane_copy(k, i, 1, direct, first).start()

    def gather(k):
        total = both(k, 0, here.across)
        for i in (1, 2, 3):
            cross_copy(k, i, here.order[i], here.z).wait_recv()
            place = 1 + lax.rem(here.order[i] - here.z + 3, 4)
            total = total + from_plane[k, place].astype(jnp.float32)
        mine(k, 0, here.across)[...] = total.astype(jnp.bfloat16)
        plane_copy(k, 0, 0, here.across, links(k, 0)[0]).start()

    def pass_on(k, i):
        first, second, _, onward = links(k, i)
        total = both(k, i, onward)
        if k not in GATHER or i == 0:
            plane_copy(k, i, 0, onward, first).wait_recv()
            total = total + from_plane[k, i].astype(jnp.float32)
        mine(k, i, onward)[...] = total.astype(jnp.bfloat16)
        plane_copy(k, i, 2, onward, second).start()

    def line_copy(k, i, source):
        return pltpu.make_async_remote_copy(
            src_ref=mine(k, i, here.own),
            dst_ref=from_line.at[k, source],
            send_sem=line_send.at[k, max(i, 1) - 1],
            recv_sem=line_recv.at[k, source],
            device_id=here.peers[max(i, 1) - 1],
            device_id_type=MESH,
        )

    def line_sum(k, i):
        first, second, _, _ = links(k, i)
        plane_copy(k, i, 1, here.own, first).wait_recv()
        plane_copy(k, i, 2, here.own, second).wait_recv()
        total = both(k, i, here.own) + from_plane[k, 4 + i].astype(jnp.float32)
        return total + from_plane[k, 8 + i].astype(jnp.float32)

    def send_line(k, i):
        mine(k, i, here.own)[...] = line_sum(k, i).astype(jnp.bfloat16)
        line_copy(k, i, here.z).start()

    def finish(k):
        tokens = pl.ds(pl.multiple_of(k * size, size), size)
        total = hidden[tokens, :] + line_sum(k, 0)
        for source in here.order[1:]:
            line_copy(k, 0, source).wait_recv()
            total = total + from_line[k, source].astype(jnp.float32)
        out_ref[tokens, :] = total.astype(jnp.bfloat16)

    def sums_sent(k):
        for i in range(4):
            core_copy(k, i).wait_send()
            for kind in range(3):
                plane_copy(k, i, kind, here.own, here.to_x).wait_send()
        for i in range(1, 4):
            line_copy(k, i, 0).wait_send()

    def send_core(k):
        for i in (3, 2, 1, 0):
            core_copy(k, i).start()

    moves = (
        lambda k, i: send_peers(k),
        along_line,
        beside,
        across,
        lambda k, i: all_rows(k),
        leave,
        pass_on,
        send_line,
        lambda k, i: finish(k),
        lambda k, i: send_core(k),
        lambda k, i: send_last(k),
        lambda k, i: pass_last(k),
        lambda k, i: gather(k),
    )

    def run(events):
        for event in events:
            moves[event // 100](event // 10 % 10, event % 10)

    tiles = units // 256
    steps = 2 * tiles + 2
    run(SCHEDULE[0])
    for copy in loads:
        copy.wait()

    @pl.loop(0, chunks)
    def _(k):
        for n in range(steps):
            if n < 2 * tiles:
                activate(k, core if n < tiles else 1 - core, n % tiles)
            elif n == 2 * tiles:
                for chunk in range(chunks):
                    pl.when(k == chunk)(functools.partial(rows_sent, chunk))
                lower(k, 1 - core)
            else:
                lower(k, core)
            for chunk in range(chunks):
                events = SCHEDULE[1 + chunk * steps + n]
                if events:
                    pl.when(k == chunk)(functools.partial(run, events))

    for k in range(chunks):
        sums_sent(k)
    for i in (1, 2, 3):
        for n in range(3):
            head_copy(n, i, here.z).wait_send()
        part_copy(0, i, None, here.z, False).wait_send()
        for g in (1, 2, 3):
            for k in range(chunks):
                part_copy(g, i, k, here.z, False).wait_send()


def local_block(
    queries,
    key_heads,
    value_heads,
    residual,
    lengths,
    routes,
    gate_weights,
    out_weight,
    norm_gain,
    w_gate,
    w_up,
    w_down,
):
    tokens, width = residual.shape[1:]
    line, size = lax.axis_size("seq"), ROWS
    chunks = tokens // size
    units = w_gate.shape[3]
    anywhere = pl.BlockSpec(memory_space=pl.ANY)
    inside = pl.BlockSpec(memory_space=pltpu.VMEM)
    scalars = pl.BlockSpec(memory_space=pltpu.SMEM)
    dma = pltpu.SemaphoreType.DMA
    half = jnp.bfloat16
    head_width, key_width = queries.shape[2] // line, key_heads.shape[2] // line
    whole = line * tokens
    result = pl.pallas_call(
        functools.partial(block_kernel, chunks, size),
        out_shape=jax.ShapeDtypeStruct((tokens, width), half),
        in_specs=[
            anywhere,
            anywhere,
            anywhere,
            inside,
            scalars,
            inside,
            inside,
            anywhere,
            inside,
            anywhere,
            anywhere,
            anywhere,
        ],
        out_specs=inside,
        scratch_shapes=[
            pltpu.VMEM((whole, head_width), half),
            pltpu.VMEM((whole, key_width), half),
            pltpu.VMEM((whole, key_width), half),
            pltpu.VMEM((whole, head_width), half),
            pltpu.VMEM((whole, width), half),
            pltpu.VMEM((line, tokens, width), half),
            pltpu.VMEM((tokens, width), half),
            pltpu.VMEM((tokens, width), jnp.float32),
            pltpu.VMEM((chunks, 32 * size, width + 128), half),
            pltpu.VMEM((chunks, 4, 4 * size, width), half),
            pltpu.VMEM((chunks, 12, size, width), half),
            pltpu.VMEM((chunks, 4, size, width), half),
            pltpu.VMEM(w_gate.shape[2:], half),
            pltpu.VMEM(w_up.shape[2:], half),
            pltpu.VMEM(w_down.shape[2:], half),
            pltpu.VMEM((32 * size, units), half),
            dma((10,)),
            dma((3, 3)),
            dma((3, line)),
            dma((28,)),
            dma((32,)),
            dma((3, 1 + 3 * chunks)),
            dma((line, 1 + 3 * chunks)),
            dma((1 + 3 * chunks,)),
            dma((chunks, 36)),
            dma((chunks, 32)),
            dma((chunks, 4)),
            dma((chunks, 4)),
            dma((chunks, 12)),
            dma((chunks, 12)),
            dma((chunks, 3)),
            dma((chunks, 4)),
        ],
        compiler_params=pltpu.CompilerParams(
            collective_id=0, has_side_effects=True, vmem_limit_bytes=67_000_000
        ),
    )(
        queries[0],
        key_heads[0],
        value_heads[0],
        residual[0],
        lengths,
        routes[0].T,
        gate_weights[0].T,
        out_weight,
        norm_gain[None, :],
        w_gate[0, 0],
        w_up[0, 0],
        w_down[0, 0],
    )
    return result[None]


def solution(mesh):
    plane = mesh.shape["exp"] == 8 and mesh.shape["seq"] == 4

    def local(*arguments):
        dense = plane and arguments[3].shape[1] == CHUNKS * ROWS
        return (local_block if dense else local_routed)(*arguments)

    return jax.shard_map(
        local,
        mesh=mesh,
        in_specs=(
            P("exp", "seq", None),
            P("exp", "seq", None),
            P("exp", "seq", None),
            P("exp", "seq", None),
            P("exp", None),
            P("exp", "seq", None),
            P("exp", "seq", None),
            P("seq", "exp"),
            P(),
            P("exp", "seq", None, None),
            P("exp", "seq", None, None),
            P("exp", "seq", None, None),
        ),
        out_specs=P("exp", "seq", None),
        check_vma=False,
    )
```
